256 devices in a mesh: dp: 16 (over z, x_hi), shard: 16 (over x_lo, y, core).
Axes of the slice: x: 4 (x_hi: 2, x_lo: 2; x = x_hi * 2 + x_lo), y: 4, z: 8, core: 2. Of those that a mesh axis runs over, the one named last changes fastest.
Arguments:
- tokens: bfloat16 [16384, 2048], P(('dp', 'shard')), may hold values from -6 to 6
- router_probs: float32 [16384, 8], P(('dp', 'shard')), may hold values from 0.05 to 1
- expert_ids: int32 [16384, 8], P(('dp', 'shard')), may hold values from 0 to 31, all different within a row; in each aligned block of 64 rows (0 to 63, 64 to 127, ...) at most 32 rows name the same one
- old_place: int32 [32], replicated, may hold values from 0 to 31, as said below
- new_place: int32 [32], replicated, may hold values from 0 to 31, as said below
- w_gate: bfloat16 [32, 2048, 1024], P('dp', 'shard'), may hold values from -0.125 to 0.125
- w_up: bfloat16 [32, 2048, 1024], P('dp', 'shard'), may hold values from -0.125 to 0.125
- w_down: bfloat16 [32, 2048, 1024], P('dp', 'shard'), may hold values from -0.1875 to 0.1875
Outputs:
- moe_output: bfloat16 [16384, 2048], P(('dp', 'shard'))
- new_gate: bfloat16 [32, 2048, 1024], P('dp', 'shard')
- new_up: bfloat16 [32, 2048, 1024], P('dp', 'shard')
- new_down: bfloat16 [32, 2048, 1024], P('dp', 'shard')
The draws below stay inside these ranges and needn't reach their ends.
Inputs may be any that keep to these rules, and one draw needn't show every extreme that they name: `expert_ids`: each token names 8 different experts; among the tokens of one device no expert is named by more than 32 tokens, a bound that some block reaches. `old_place`: a permutation of the 32 experts over the 32 slots. `new_place`: equal to old_place except at exactly one of the slots 2 k and 2 k + 1 for each k; the expert leaving the refilled slot of k moves to the refilled slot of (k + 1) mod (16), so that new_place is again a permutation.
All inputs are finite; a program needn't handle non-finite values.
Results may differ from the reference program's by a relative error of at most 0.0064.
Values may be sent and summed in bfloat16 or wider, within the bound.
A program may use at most 128 MiB of HBM per device.

```python
import math
import jax
import jax.numpy as jnp
import numpy as np
from jax import lax

D = 2048
FF = 1024
TOP = 8
TOK_DEV = 64
SLOTS = 32
EXPERTS = 32
CAP = 32
TOKENS = 16384


def placements(key):
    row_total = SLOTS // 2
    old_slots = jax.random.permutation(jax.random.fold_in(key, 11), SLOTS).astype(jnp.int32)
    chosen = jax.random.randint(jax.random.fold_in(key, 12), (row_total,), 0, 2).astype(jnp.int32)
    refilled = 2 * jnp.arange(row_total, dtype=jnp.int32) + chosen
    target_row = ((jnp.arange(row_total, dtype=jnp.int32) + 1) % row_total).astype(jnp.int32)
    new_slots = old_slots.at[refilled[target_row]].set(old_slots[refilled])
    return (old_slots, new_slots)


def draw_old_place(key, part):
    return placements(key)[0]


def draw_new_place(key, part):
    return placements(key)[1]


def steps_of(rng, shape, cuts, low, top_value):
    def one(position, shards_of):
        draws = jax.random.uniform(jax.random.fold_in(jax.random.fold_in(rng, 6), position), (shards_of,), jnp.float32, low / len(cuts), top_value / len(cuts))
        return jnp.repeat(jnp.exp(draws), shape[position] // shards_of).reshape((-1,) + (1,) * (len(shape) - position - 1))

    gain = one(*cuts[0])
    for cut in cuts[1:]:
        gain = gain * one(*cut)
    return gain


def routed_block(stream_key, own, number, rows, number_of, top, limit, lean):
    ranking = jax.random.permutation(stream_key, number_of)
    heavy_load, usual = load_shares(number_of, rows * top, limit, lean, True), load_shares(number_of, rows * top, limit, lean, False)
    places = jnp.arange(number_of)

    def named(lengths, turn):
        used = int((lengths > 0).sum())
        fixed = max(1, used // 4)
        moved = fixed + (places - fixed + turn * (used - fixed)) % max(1, number_of - fixed)
        return jnp.zeros((number_of,), jnp.int32).at[ranking[jnp.where(places < fixed, places, moved)]].set(jnp.asarray(lengths, jnp.int32))

    lengths = jnp.where(number % 4 == 0, named(heavy_load, number // 4), named(usual, number - number // 4 - 1))
    mixed = jax.random.permutation(jax.random.fold_in(own, 3), number_of)
    donor, sink = mixed[0:number_of // 2 * 2:2], mixed[1:number_of // 2 * 2:2]
    slack = jnp.minimum(lengths[donor] - 1, limit - lengths[sink]) // 2
    slack = jnp.where((donor == ranking[0]) | (sink == ranking[0]) | (lengths[sink] == 0), 0, jnp.maximum(slack, 0))
    moved = jax.random.randint(jax.random.fold_in(own, 4), (number_of // 2,), 0, 1 << 20) % (slack + 1)
    lengths = lengths.at[donor].add(-moved).at[sink].add(moved)
    items = jnp.searchsorted(jnp.cumsum(lengths), jnp.arange(rows * top), side="right").astype(jnp.int32)
    table = items.reshape(top, rows).T
    table = table[jax.random.permutation(jax.random.fold_in(own, 1), rows)]
    turn = jax.random.randint(jax.random.fold_in(own, 2), (rows, 1), 0, top)
    return jnp.take_along_axis(table, (jnp.arange(top)[None, :] + turn) % top, axis=1)


def load_shares(amount, total, reach, lean, full):
    loads = [(1 << 20) // math.isqrt(grade ** lean) + 1 for grade in range(1, amount + 1)]
    largest = reach if full else min(reach, max(-(-total // amount), total * loads[0] // sum(loads)))
    least = 1 if total - largest >= amount - 1 else 0
    holding, surplus = [largest] + [least] * (amount - 1), total - largest - least * (amount - 1)
    while surplus > 0:
        free = [i for i in range(1, amount) if holding[i] < largest] or [i for i in range(1, amount) if holding[i] < reach]
        mass, budget = sum([loads[i] for i in free]), surplus
        for i in free:
            more = min(reach - holding[i], max(1, budget * loads[i] // mass), surplus)
            holding[i] = holding[i] + more
            surplus = surplus - more
    return np.array(holding)


def centred(rng, extent, deviation, limit, cuts=(), kind=jnp.bfloat16):
    factor_of = steps_of(rng, extent, cuts, -0.22, 0.18) if cuts else 1.0
    entries = jax.random.normal(rng, extent, jnp.float32) * deviation * factor_of
    return jnp.minimum(jnp.maximum(entries, -limit), limit).astype(kind)


def setup_inputs(seed: int = 0) -> dict:
    key_list = jax.random.split(jax.random.key(seed), 9)
    tokens = centred(key_list[0], (TOKENS, D), 1.0, 6.0, ((0, 256),))
    router_probs = jnp.clip(jnp.exp(math.log(1.0) - 2.9957323 * jax.random.uniform(key_list[1], (TOKENS, TOP), jnp.float32) ** steps_of(key_list[1], (TOKENS, TOP), ((0, 256),), -0.2, 0.2)), 0.05, 1.0)
    expert_ids_keys = jax.random.split(jax.random.fold_in(key_list[2], 1), TOKENS // TOK_DEV)
    expert_ids_turns = jax.random.permutation(jax.random.fold_in(key_list[2], 3), TOKENS // TOK_DEV)
    expert_ids = jax.vmap(lambda own, number: routed_block(jax.random.fold_in(key_list[2], 2), own, number, TOK_DEV, EXPERTS, TOP, CAP, 2))(expert_ids_keys, expert_ids_turns).reshape((TOKENS, TOP))
    old_place = draw_old_place(jax.random.fold_in(key_list[8], 71), 0)
    new_place = draw_new_place(jax.random.fold_in(key_list[8], 71), 0)
    w_gate = centred(key_list[5], (SLOTS, D, FF), D ** -0.5, 0.125, ((0, 16), (1, 16)))
    w_up = centred(key_list[6], (SLOTS, D, FF), D ** -0.5, 0.125, ((0, 16), (1, 16)))
    w_down = centred(key_list[7], (SLOTS, D, FF), FF ** -0.5, 0.1875, ((0, 16), (1, 16)))
    return {"tokens": tokens, "router_probs": router_probs, "expert_ids": expert_ids, "old_place": old_place, "new_place": new_place, "w_gate": w_gate, "w_up": w_up, "w_down": w_down}


def reference(tokens, router_probs, expert_ids, old_place, new_place, w_gate, w_up, w_down):
    pair_count = TOKENS * TOP
    block_rows = 512
    slot_index = jnp.arange(SLOTS, dtype=jnp.int32)
    expert_index = jnp.arange(EXPERTS, dtype=jnp.int32)
    owner_slot = jnp.sum(jnp.where(old_place[None, :] == expert_index[:, None], slot_index[None, :], 0), axis=1).astype(jnp.int32)
    slot_ids = owner_slot[expert_ids].reshape(-1).astype(jnp.int32)
    gate_weights = (router_probs / jnp.sum(router_probs, axis=1, keepdims=True)).astype(jnp.bfloat16).reshape(-1)
    order = jnp.argsort(slot_ids * pair_count + jnp.arange(pair_count, dtype=jnp.int32)).astype(jnp.int32)
    counts = jnp.zeros((SLOTS,), jnp.int32).at[slot_ids].add(1)
    starts = (jnp.cumsum(counts) - counts).astype(jnp.int32)
    padded = jnp.concatenate([order, jnp.zeros((block_rows,), jnp.int32)])
    total = jnp.zeros((TOKENS, D), jnp.float32)

    def slot_step(slot, total):
        slot = jnp.asarray(slot).astype(jnp.int32)

        def block_step(block, total):
            block = jnp.asarray(block).astype(jnp.int32)
            begin = (starts[slot] + block * block_rows).astype(jnp.int32)
            pairs = lax.dynamic_slice_in_dim(padded, begin, block_rows)
            live = (jnp.arange(block_rows, dtype=jnp.int32) + block * block_rows) < counts[slot]
            token_rows = tokens[pairs // TOP]
            gate_part = jnp.dot(token_rows, w_gate[slot], preferred_element_type=jnp.float32)
            up_part = jnp.dot(token_rows, w_up[slot], preferred_element_type=jnp.float32)
            hidden = (jax.nn.silu(gate_part) * up_part).astype(jnp.bfloat16)
            result = lax.dot_general(hidden, w_down[slot], (((1,), (1,)), ((), ())), preferred_element_type=jnp.float32).astype(jnp.bfloat16)
            weight = jnp.where(live, gate_weights[pairs].astype(jnp.float32), jnp.float32(0.0))
            return total.at[pairs // TOP].add(result.astype(jnp.float32) * weight[:, None])

        block_total = ((counts[slot] + block_rows - 1) // block_rows).astype(jnp.int32)
        return lax.fori_loop(jnp.int32(0), block_total, block_step, total)

    total = lax.fori_loop(0, SLOTS, slot_step, total)
    moe_output = total.astype(jnp.bfloat16)
    source = owner_slot[new_place]
    return (moe_output, w_gate[source], w_up[source], w_down[source])
```

```python
import jax
import jax.numpy as jnp
from jax import lax
from jax.sharding import PartitionSpec as P


def partner_2(x, axis, apart):
    return lax.ppermute(x, axis, [(i, i ^ 1 << apart) for i in range(lax.axis_size(axis))])


def passed_along(x, axis, by):
    size = lax.axis_size(axis)
    return lax.ppermute(x, axis, [(i, (i + by) % size) for i in range(size)])


def lookup(lookup_keys, lookup_table, entry_count):
    matches = lookup_keys[..., None] == jnp.arange(entry_count, dtype=jnp.int32)
    return jnp.sum(jnp.where(matches, lookup_table, 0), axis=-1)


def widen(pieces, half_count):
    return jnp.repeat(pieces, half_count, axis=0)


def pair_halves(upper_half, own_rows, other_rows):
    return jnp.where(
        upper_half,
        jnp.stack([other_rows, own_rows], axis=1),
        jnp.stack([own_rows, other_rows], axis=1),
    )


def local(tokens, router_probs, expert_ids, old_place, new_place, w_gate, w_up, w_down):
    slot_count = old_place.shape[0]
    tok_count, top_count = expert_ids.shape
    model_width = tokens.shape[1]
    n_shard = lax.axis_size("shard")
    half_count = n_shard // 2
    partner_bit = n_shard.bit_length() - 2
    column = lax.axis_index("shard")
    row_id = lax.axis_index("dp")
    n_rows = lax.axis_size("dp")
    upper_half = column >= half_count
    capacity = max(2, 2 * tok_count * top_count // slot_count)
    places = slot_count * capacity
    full_gate, full_up, full_down = (
        lax.all_to_all(widen(w_gate, half_count), "shard", split_axis=0, concat_axis=1, tiled=True),
        lax.all_to_all(widen(w_up, half_count), "shard", split_axis=0, concat_axis=1, tiled=True),
        lax.all_to_all(widen(w_down, half_count), "shard", split_axis=0, concat_axis=1, tiled=True),
    )
    full_gate = full_gate[0]
    full_up = full_up[0]
    full_down = full_down[0]
    slot_index = jnp.arange(slot_count, dtype=jnp.int32)
    owner_slot = jnp.sum(
        jnp.where(old_place[None, :] == slot_index[:, None], slot_index[None, :], 0), axis=1
    )
    slot_ids = lookup(expert_ids, owner_slot, slot_count)
    gate_weights = (router_probs / jnp.sum(router_probs, axis=1, keepdims=True)).astype(
        jnp.bfloat16
    )
    flat_slots = slot_ids.reshape(-1)
    members = (flat_slots[:, None] == slot_index[None, :]).astype(jnp.int32)
    earlier = jnp.cumsum(members, axis=0) - members
    slot_rank = jnp.sum(earlier * members, axis=1)
    position = (flat_slots * capacity + slot_rank).reshape(tok_count, top_count)
    matches = position[:, :, None] == jnp.arange(places, dtype=jnp.int32)[None, None, :]
    gathered_tokens = lax.all_gather(tokens, "dp", axis=0, tiled=False)
    gathered_ids = lax.all_gather(expert_ids, "dp", axis=0, tiled=False)
    gathered_slots = lookup(gathered_ids, owner_slot, slot_count).reshape(n_rows, -1)
    row_slots = 2 * row_id + jnp.arange(2, dtype=jnp.int32)
    in_row = (gathered_slots[:, :, None] == row_slots[None, None, :]).astype(jnp.int32)
    row_rank = jnp.cumsum(in_row, axis=1) - in_row
    picks = (in_row[..., None] == 1) & (
        row_rank[..., None] == jnp.arange(capacity, dtype=jnp.int32)
    )
    picks = jnp.any(picks.reshape(n_rows, tok_count, top_count, 2, capacity), axis=2)
    arrived = jnp.einsum(
        "stcr,std->scrd",
        picks.astype(jnp.bfloat16),
        gathered_tokens,
        preferred_element_type=jnp.float32,
    ).astype(jnp.bfloat16)
    own_rows = jnp.where(upper_half, arrived[:, 1], arrived[:, 0])
    other_rows = jnp.where(upper_half, arrived[:, 0], arrived[:, 1])
    partner = partner_2(other_rows, "shard", partner_bit)
    work_rows = jnp.stack([own_rows, partner], axis=0)
    flat_rows = work_rows.reshape(-1, model_width)
    gate_part = jnp.dot(flat_rows, full_gate, preferred_element_type=jnp.float32)
    up_part = jnp.dot(flat_rows, full_up, preferred_element_type=jnp.float32)
    hidden = (jax.nn.silu(gate_part) * up_part).astype(jnp.bfloat16)
    result = lax.dot_general(
        hidden, full_down, (((1,), (1,)), ((), ())), preferred_element_type=jnp.float32
    ).astype(jnp.bfloat16)
    result = result.reshape(2, n_rows, capacity, model_width)
    returned_other = partner_2(result[1], "shard", partner_bit)
    returned = lax.all_to_all(
        pair_halves(upper_half, result[0], returned_other),
        "dp",
        split_axis=0,
        concat_axis=0,
        tiled=True,
    )
    combine = jnp.sum(
        jnp.where(matches, gate_weights[:, :, None], jnp.zeros((), jnp.bfloat16)), axis=1
    )
    moe_output = jnp.dot(
        combine, returned.reshape(places, model_width), preferred_element_type=jnp.float32
    ).astype(jnp.bfloat16)
    base_slot = 2 * row_id
    second_old = lax.dynamic_index_in_dim(old_place, base_slot + 1, 0, keepdims=False)
    second_new = lax.dynamic_index_in_dim(new_place, base_slot + 1, 0, keepdims=False)
    second_moved = second_new != second_old
    leave_gate = jnp.where(second_moved, w_gate[1], w_gate[0])
    leave_up = jnp.where(second_moved, w_up[1], w_up[0])
    leave_down = jnp.where(second_moved, w_down[1], w_down[0])
    arrive_gate, arrive_up, arrive_down = passed_along((leave_gate, leave_up, leave_down), "dp", 1)
    new_gate = jnp.stack(
        [
            jnp.where(second_moved, w_gate[0], arrive_gate),
            jnp.where(second_moved, arrive_gate, w_gate[1]),
        ],
        axis=0,
    )
    new_up = jnp.stack(
        [jnp.where(second_moved, w_up[0], arrive_up), jnp.where(second_moved, arrive_up, w_up[1])],
        axis=0,
    )
    new_down = jnp.stack(
        [
            jnp.where(second_moved, w_down[0], arrive_down),
            jnp.where(second_moved, arrive_down, w_down[1]),
        ],
        axis=0,
    )
    return (moe_output, new_gate, new_up, new_down)


def solution(mesh):
    in_specs = (
        P(("dp", "shard"), None),
        P(("dp", "shard"), None),
        P(("dp", "shard"), None),
        P(),
        P(),
        P("dp", "shard", None),
        P("dp", "shard", None),
        P("dp", "shard", None),
    )
    out_specs = (
        P(("dp", "shard"), None),
        P("dp", "shard", None),
        P("dp", "shard", None),
        P("dp", "shard", None),
    )
    return jax.shard_map(local, mesh=mesh, in_specs=in_specs, out_specs=out_specs, check_vma=False)
```

```python
import jax
import jax.numpy as jnp
from jax import lax
from jax.sharding import PartitionSpec as P


def partner_2(x, axis, apart):
    return lax.ppermute(x, axis, [(i, i ^ 1 << apart) for i in range(lax.axis_size(axis))])


def passed_along(x, axis, by):
    size = lax.axis_size(axis)
    return lax.ppermute(x, axis, [(i, (i + by) % size) for i in range(size)])


def lookup(lookup_keys, lookup_table, entry_count):
    matches = lookup_keys[..., None] == jnp.arange(entry_count, dtype=jnp.int32)
    return jnp.sum(jnp.where(matches, lookup_table, 0), axis=-1)


def widen(pieces, half_count):
    return jnp.tile(pieces, (half_count, 1, 1))


def pair_halves(upper_half, own_rows, other_rows):
    return jnp.where(
        upper_half,
        jnp.stack([other_rows, own_rows], axis=1),
        jnp.stack([own_rows, other_rows], axis=1),
    )


def local(tokens, router_probs, expert_ids, old_place, new_place, w_gate, w_up, w_down):
    slot_count = old_place.shape[0]
    tok_count, top_count = expert_ids.shape
    model_width = tokens.shape[1]
    n_shard = lax.axis_size("shard")
    half_count = n_shard // 2
    column = lax.axis_index("shard")
    row_id = lax.axis_index("dp")
    n_rows = lax.axis_size("dp")
    upper_half = column % 2 == 1
    capacity = max(2, 2 * tok_count * top_count // slot_count)
    places = slot_count * capacity
    full_gate, full_up, full_down = (
        lax.all_to_all(widen(w_gate, half_count), "shard", split_axis=0, concat_axis=1, tiled=True),
        lax.all_to_all(widen(w_up, half_count), "shard", split_axis=0, concat_axis=1, tiled=True),
        lax.all_to_all(widen(w_down, half_count), "shard", split_axis=0, concat_axis=1, tiled=True),
    )
    full_gate = full_gate[0]
    full_up = full_up[0]
    full_down = full_down[0]
    slot_index = jnp.arange(slot_count, dtype=jnp.int32)
    owner_slot = jnp.sum(
        jnp.where(old_place[None, :] == slot_index[:, None], slot_index[None, :], 0), axis=1
    )
    slot_ids = lookup(expert_ids, owner_slot, slot_count)
    gate_weights = (router_probs / jnp.sum(router_probs, axis=1, keepdims=True)).astype(
        jnp.bfloat16
    )
    flat_slots = slot_ids.reshape(-1)
    members = (flat_slots[:, None] == slot_index[None, :]).astype(jnp.int32)
    earlier = jnp.cumsum(members, axis=0) - members
    slot_rank = jnp.sum(earlier * members, axis=1)
    position = (flat_slots * capacity + slot_rank).reshape(tok_count, top_count)
    matches = position[:, :, None] == jnp.arange(places, dtype=jnp.int32)[None, None, :]
    gathered_tokens = lax.all_gather(tokens, "dp", axis=0, tiled=False)
    gathered_ids = lax.all_gather(expert_ids, "dp", axis=0, tiled=False)
    gathered_slots = lookup(gathered_ids, owner_slot, slot_count).reshape(n_rows, -1)
    row_slots = 2 * row_id + jnp.arange(2, dtype=jnp.int32)
    in_row = (gathered_slots[:, :, None] == row_slots[None, None, :]).astype(jnp.int32)
    row_rank = jnp.cumsum(in_row, axis=1) - in_row
    picks = (in_row[..., None] == 1) & (
        row_rank[..., None] == jnp.arange(capacity, dtype=jnp.int32)
    )
    picks = jnp.any(picks.reshape(n_rows, tok_count, top_count, 2, capacity), axis=2)
    arrived = jnp.einsum(
        "stcr,std->scrd",
        picks.astype(jnp.bfloat16),
        gathered_tokens,
        preferred_element_type=jnp.float32,
    ).astype(jnp.bfloat16)
    own_rows = jnp.where(upper_half, arrived[:, 1], arrived[:, 0])
    other_rows = jnp.where(upper_half, arrived[:, 0], arrived[:, 1])
    partner = partner_2(other_rows, "shard", 0)
    work_rows = jnp.stack([own_rows, partner], axis=0)
    flat_rows = work_rows.reshape(-1, model_width)
    gate_part = jnp.dot(flat_rows, full_gate, preferred_element_type=jnp.float32)
    up_part = jnp.dot(flat_rows, full_up, preferred_element_type=jnp.float32)
    hidden = (jax.nn.silu(gate_part) * up_part).astype(jnp.bfloat16)
    result = lax.dot_general(
        hidden, full_down, (((1,), (1,)), ((), ())), preferred_element_type=jnp.float32
    ).astype(jnp.bfloat16)
    result = result.reshape(2, n_rows, capacity, model_width)
    returned_other = partner_2(result[1], "shard", 0)
    returned = lax.all_to_all(
        pair_halves(upper_half, result[0], returned_other),
        "dp",
        split_axis=0,
        concat_axis=0,
        tiled=True,
    )
    combine = jnp.sum(
        jnp.where(matches, gate_weights[:, :, None], jnp.zeros((), jnp.bfloat16)), axis=1
    )
    moe_output = jnp.dot(
        combine, returned.reshape(places, model_width), preferred_element_type=jnp.float32
    ).astype(jnp.bfloat16)
    base_slot = 2 * row_id
    second_old = lax.dynamic_index_in_dim(old_place, base_slot + 1, 0, keepdims=False)
    second_new = lax.dynamic_index_in_dim(new_place, base_slot + 1, 0, keepdims=False)
    second_moved = second_new != second_old
    leave_gate = jnp.where(second_moved, w_gate[1], w_gate[0])
    leave_up = jnp.where(second_moved, w_up[1], w_up[0])
    leave_down = jnp.where(second_moved, w_down[1], w_down[0])
    arrive_gate, arrive_up, arrive_down = passed_along((leave_gate, leave_up, leave_down), "dp", 1)
    new_gate = jnp.stack(
        [
            jnp.where(second_moved, w_gate[0], arrive_gate),
            jnp.where(second_moved, arrive_gate, w_gate[1]),
        ],
        axis=0,
    )
    new_up = jnp.stack(
        [jnp.where(second_moved, w_up[0], arrive_up), jnp.where(second_moved, arrive_up, w_up[1])],
        axis=0,
    )
    new_down = jnp.stack(
        [
            jnp.where(second_moved, w_down[0], arrive_down),
            jnp.where(second_moved, arrive_down, w_down[1]),
        ],
        axis=0,
    )
    return (moe_output, new_gate, new_up, new_down)


def solution(mesh):
    in_specs = (
        P(("dp", "shard"), None),
        P(("dp", "shard"), None),
        P(("dp", "shard"), None),
        P(),
        P(),
        P("dp", "shard", None),
        P("dp", "shard", None),
        P("dp", "shard", None),
    )
    out_specs = (
        P(("dp", "shard"), None),
        P("dp", "shard", None),
        P("dp", "shard", None),
        P("dp", "shard", None),
    )
    return jax.shard_map(local, mesh=mesh, in_specs=in_specs, out_specs=out_specs, check_vma=False)
```

```python
import jax
import jax.numpy as jnp
from jax import lax
from jax.sharding import PartitionSpec as P


def partner_2(x, axis, apart):
    return lax.ppermute(x, axis, [(i, i ^ 1 << apart) for i in range(lax.axis_size(axis))])


def passed_along(x, axis, by):
    size = lax.axis_size(axis)
    return lax.ppermute(x, axis, [(i, (i + by) % size) for i in range(size)])


def lookup(lookup_keys, lookup_table, entry_count):
    matches = lookup_keys[..., None] == jnp.arange(entry_count, dtype=jnp.int32)
    return jnp.sum(jnp.where(matches, lookup_table, 0), axis=-1)


def widen(pieces, half_count):
    return jnp.tile(pieces, (half_count, 1, 1))


def pair_halves(upper_half, own_rows, other_rows):
    return jnp.where(
        upper_half,
        jnp.stack([other_rows, own_rows], axis=1),
        jnp.stack([own_rows, other_rows], axis=1),
    )


def local(tokens, router_probs, expert_ids, old_place, new_place, w_gate, w_up, w_down):
    slot_count = old_place.shape[0]
    tok_count, top_count = expert_ids.shape
    model_width = tokens.shape[1]
    n_shard = lax.axis_size("shard")
    half_count = n_shard // 2
    column = lax.axis_index("shard")
    row_id = lax.axis_index("dp")
    n_rows = lax.axis_size("dp")
    upper_half = column % 2 == 1
    capacity = max(2, 2 * tok_count * top_count // slot_count)
    places = slot_count * capacity
    full_gate, full_up, full_down = (
        lax.all_to_all(widen(w_gate, half_count), "shard", split_axis=0, concat_axis=1, tiled=True),
        lax.all_to_all(widen(w_up, half_count), "shard", split_axis=0, concat_axis=1, tiled=True),
        lax.all_to_all(widen(w_down, half_count), "shard", split_axis=0, concat_axis=1, tiled=True),
    )
    full_gate = full_gate[0]
    full_up = full_up[0]
    full_down = full_down[0]
    slot_index = jnp.arange(slot_count, dtype=jnp.int32)
    owner_slot = jnp.sum(
        jnp.where(old_place[None, :] == slot_index[:, None], slot_index[None, :], 0), axis=1
    )
    slot_ids = lookup(expert_ids, owner_slot, slot_count)
    gate_weights = (router_probs / jnp.sum(router_probs, axis=1, keepdims=True)).astype(
        jnp.bfloat16
    )
    side = jnp.concatenate(
        [
            slot_ids.astype(jnp.bfloat16),
            gate_weights,
            jnp.zeros((tok_count, 128 - 2 * top_count), jnp.bfloat16),
        ],
        axis=1,
    )
    gathered = lax.all_gather(jnp.concatenate([tokens, side], axis=1), "dp", axis=0, tiled=False)
    gathered_tokens = gathered[..., :model_width]
    gathered_slots = (
        gathered[..., model_width : model_width + top_count].astype(jnp.int32).reshape(n_rows, -1)
    )
    gathered_gates = gathered[..., model_width + top_count : model_width + 2 * top_count]
    row_slots = 2 * row_id + jnp.arange(2, dtype=jnp.int32)
    in_row = (gathered_slots[:, :, None] == row_slots[None, None, :]).astype(jnp.int32)
    row_rank = jnp.cumsum(in_row, axis=1) - in_row
    picks = (in_row[..., None] == 1) & (
        row_rank[..., None] == jnp.arange(capacity, dtype=jnp.int32)
    )
    picks = picks.reshape(n_rows, tok_count, top_count, 2, capacity)
    weights = jnp.sum(
        jnp.where(picks, gathered_gates[..., None, None], jnp.zeros((), jnp.bfloat16)), axis=2
    )
    picks = jnp.any(picks, axis=2)
    arrived = jnp.einsum(
        "stcr,std->scrd",
        picks.astype(jnp.bfloat16),
        gathered_tokens,
        preferred_element_type=jnp.float32,
    ).astype(jnp.bfloat16)
    own_rows = jnp.where(upper_half, arrived[:, 1], arrived[:, 0])
    other_rows = jnp.where(upper_half, arrived[:, 0], arrived[:, 1])
    partner = partner_2(other_rows, "shard", 0)
    work_rows = jnp.stack([own_rows, partner], axis=0)
    flat_rows = work_rows.reshape(-1, model_width)
    gate_part = jnp.dot(flat_rows, full_gate, preferred_element_type=jnp.float32)
    up_part = jnp.dot(flat_rows, full_up, preferred_element_type=jnp.float32)
    hidden = (jax.nn.silu(gate_part) * up_part).astype(jnp.bfloat16)
    result = lax.dot_general(
        hidden, full_down, (((1,), (1,)), ((), ())), preferred_element_type=jnp.float32
    ).astype(jnp.bfloat16)
    result = result.reshape(2, n_rows, capacity, model_width)
    returned_other = partner_2(result[1], "shard", 0)
    partial = jnp.einsum(
        "stcr,scrd->std",
        weights,
        pair_halves(upper_half, result[0], returned_other),
        preferred_element_type=jnp.float32,
    ).astype(jnp.bfloat16)
    moe_output = lax.psum_scatter(partial, "dp", scatter_dimension=0, tiled=True)[0]
    base_slot = 2 * row_id
    second_old = lax.dynamic_index_in_dim(old_place, base_slot + 1, 0, keepdims=False)
    second_new = lax.dynamic_index_in_dim(new_place, base_slot + 1, 0, keepdims=False)
    second_moved = second_new != second_old
    leave_gate = jnp.where(second_moved, w_gate[1], w_gate[0])
    leave_up = jnp.where(second_moved, w_up[1], w_up[0])
    leave_down = jnp.where(second_moved, w_down[1], w_down[0])
    arrive_gate, arrive_up, arrive_down = passed_along((leave_gate, leave_up, leave_down), "dp", 1)
    new_gate = jnp.stack(
        [
            jnp.where(second_moved, w_gate[0], arrive_gate),
            jnp.where(second_moved, arrive_gate, w_gate[1]),
        ],
        axis=0,
    )
    new_up = jnp.stack(
        [jnp.where(second_moved, w_up[0], arrive_up), jnp.where(second_moved, arrive_up, w_up[1])],
        axis=0,
    )
    new_down = jnp.stack(
        [
            jnp.where(second_moved, w_down[0], arrive_down),
            jnp.where(second_moved, arrive_down, w_down[1]),
        ],
        axis=0,
    )
    return (moe_output, new_gate, new_up, new_down)


def solution(mesh):
    in_specs = (
        P(("dp", "shard"), None),
        P(("dp", "shard"), None),
        P(("dp", "shard"), None),
        P(),
        P(),
        P("dp", "shard", None),
        P("dp", "shard", None),
        P("dp", "shard", None),
    )
    out_specs = (
        P(("dp", "shard"), None),
        P("dp", "shard", None),
        P("dp", "shard", None),
        P("dp", "shard", None),
    )
    return jax.shard_map(local, mesh=mesh, in_specs=in_specs, out_specs=out_specs, check_vma=False)
```

```python
import jax
import jax.numpy as jnp
from jax import lax
from jax.sharding import PartitionSpec as P


def partner_2(x, axis, apart):
    return lax.ppermute(x, axis, [(i, i ^ 1 << apart) for i in range(lax.axis_size(axis))])


def passed_along(x, axis, by):
    size = lax.axis_size(axis)
    return lax.ppermute(x, axis, [(i, (i + by) % size) for i in range(size)])


def lookup(lookup_keys, lookup_table, entry_count):
    matches = lookup_keys[..., None] == jnp.arange(entry_count, dtype=jnp.int32)
    return jnp.sum(jnp.where(matches, lookup_table, 0), axis=-1)


def widen(pieces, half_count):
    return jnp.tile(pieces, (half_count, 1, 1))


def pair_halves(upper_half, own_rows, other_rows):
    return jnp.where(
        upper_half,
        jnp.stack([other_rows, own_rows], axis=1),
        jnp.stack([own_rows, other_rows], axis=1),
    )


def local(tokens, router_probs, expert_ids, old_place, new_place, w_gate, w_up, w_down):
    slot_count = old_place.shape[0]
    tok_count, top_count = expert_ids.shape
    model_width = tokens.shape[1]
    n_shard = lax.axis_size("shard")
    half_count = n_shard // 2
    column = lax.axis_index("shard")
    row_id = lax.axis_index("dp")
    n_rows = lax.axis_size("dp")
    upper_half = column % 2 == 1
    capacity = max(2, 2 * tok_count * top_count // slot_count)
    places = slot_count * capacity
    full_gate, full_up, full_down = (
        lax.all_to_all(widen(w_gate, half_count), "shard", split_axis=0, concat_axis=1, tiled=True),
        lax.all_to_all(widen(w_up, half_count), "shard", split_axis=0, concat_axis=1, tiled=True),
        lax.all_to_all(widen(w_down, half_count), "shard", split_axis=0, concat_axis=1, tiled=True),
    )
    full_gate = full_gate[0]
    full_up = full_up[0]
    full_down = full_down[0]
    slot_index = jnp.arange(slot_count, dtype=jnp.int32)
    owner_slot = jnp.sum(
        jnp.where(old_place[None, :] == slot_index[:, None], slot_index[None, :], 0), axis=1
    )
    slot_ids = lookup(expert_ids, owner_slot, slot_count)
    gate_weights = (router_probs / jnp.sum(router_probs, axis=1, keepdims=True)).astype(
        jnp.bfloat16
    )
    side = jnp.concatenate(
        [
            slot_ids.astype(jnp.bfloat16),
            jnp.zeros((tok_count, 128 - top_count), jnp.bfloat16),
        ],
        axis=1,
    )
    gathered = lax.all_gather(jnp.concatenate([tokens, side], axis=1), "dp", axis=0, tiled=False)
    gathered_tokens = gathered[..., :model_width]
    gathered_slots = (
        gathered[..., model_width : model_width + top_count].astype(jnp.int32).reshape(n_rows, -1)
    )
    row_slots = 2 * row_id + jnp.arange(2, dtype=jnp.int32)
    in_row = (gathered_slots[:, :, None] == row_slots[None, None, :]).astype(jnp.int32)
    row_rank = jnp.cumsum(in_row, axis=1) - in_row
    picks = (in_row[..., None] == 1) & (
        row_rank[..., None] == jnp.arange(capacity, dtype=jnp.int32)
    )
    picks = picks.reshape(n_rows, tok_count, top_count, 2, capacity)
    picks = jnp.any(picks, axis=2)
    arrived = jnp.einsum(
        "stcr,std->scrd",
        picks.astype(jnp.bfloat16),
        gathered_tokens,
        preferred_element_type=jnp.float32,
    ).astype(jnp.bfloat16)
    own_rows = jnp.where(upper_half, arrived[:, 1], arrived[:, 0])
    other_rows = jnp.where(upper_half, arrived[:, 0], arrived[:, 1])
    partner = partner_2(other_rows, "shard", 0)
    work_rows = jnp.stack([own_rows, partner], axis=0)
    flat_rows = work_rows.reshape(-1, model_width)
    gate_part = jnp.dot(flat_rows, full_gate, preferred_element_type=jnp.float32)
    up_part = jnp.dot(flat_rows, full_up, preferred_element_type=jnp.float32)
    hidden = (jax.nn.silu(gate_part) * up_part).astype(jnp.bfloat16)
    result = lax.dot_general(
        hidden, full_down, (((1,), (1,)), ((), ())), preferred_element_type=jnp.float32
    ).astype(jnp.bfloat16)
    result = result.reshape(2, n_rows, capacity, model_width)
    returned_other = partner_2(result[1], "shard", 0)
    returned = lax.all_to_all(
        pair_halves(upper_half, result[0], returned_other),
        "dp",
        split_axis=0,
        concat_axis=0,
        tiled=True,
    )
    flat_slots = slot_ids.reshape(-1)
    members = (flat_slots[:, None] == slot_index[None, :]).astype(jnp.int32)
    earlier = jnp.cumsum(members, axis=0) - members
    slot_rank = jnp.sum(earlier * members, axis=1)
    position = (flat_slots * capacity + slot_rank).reshape(tok_count, top_count)
    matches = position[:, :, None] == jnp.arange(places, dtype=jnp.int32)[None, None, :]
    combine = jnp.sum(
        jnp.where(matches, gate_weights[:, :, None], jnp.zeros((), jnp.bfloat16)), axis=1
    )
    moe_output = jnp.dot(
        combine, returned.reshape(places, model_width), preferred_element_type=jnp.float32
    ).astype(jnp.bfloat16)
    base_slot = 2 * row_id
    second_old = lax.dynamic_index_in_dim(old_place, base_slot + 1, 0, keepdims=False)
    second_new = lax.dynamic_index_in_dim(new_place, base_slot + 1, 0, keepdims=False)
    second_moved = second_new != second_old
    leave_gate = jnp.where(second_moved, w_gate[1], w_gate[0])
    leave_up = jnp.where(second_moved, w_up[1], w_up[0])
    leave_down = jnp.where(second_moved, w_down[1], w_down[0])
    arrive_gate, arrive_up, arrive_down = passed_along((leave_gate, leave_up, leave_down), "dp", 1)
    new_gate = jnp.stack(
        [
            jnp.where(second_moved, w_gate[0], arrive_gate),
            jnp.where(second_moved, arrive_gate, w_gate[1]),
        ],
        axis=0,
    )
    new_up = jnp.stack(
        [jnp.where(second_moved, w_up[0], arrive_up), jnp.where(second_moved, arrive_up, w_up[1])],
        axis=0,
    )
    new_down = jnp.stack(
        [
            jnp.where(second_moved, w_down[0], arrive_down),
            jnp.where(second_moved, arrive_down, w_down[1]),
        ],
        axis=0,
    )
    return (moe_output, new_gate, new_up, new_down)


def solution(mesh):
    in_specs = (
        P(("dp", "shard"), None),
        P(("dp", "shard"), None),
        P(("dp", "shard"), None),
        P(),
        P(),
        P("dp", "shard", None),
        P("dp", "shard", None),
        P("dp", "shard", None),
    )
    out_specs = (
        P(("dp", "shard"), None),
        P("dp", "shard", None),
        P("dp", "shard", None),
        P("dp", "shard", None),
    )
    return jax.shard_map(local, mesh=mesh, in_specs=in_specs, out_specs=out_specs, check_vma=False)
```

```python
import jax
import jax.numpy as jnp
from jax import lax
from jax.sharding import PartitionSpec as P


def partner_2(x, axis, apart):
    return lax.ppermute(x, axis, [(i, i ^ 1 << apart) for i in range(lax.axis_size(axis))])


def passed_along(x, axis, by):
    size = lax.axis_size(axis)
    return lax.ppermute(x, axis, [(i, (i + by) % size) for i in range(size)])


def lookup(lookup_keys, lookup_table, entry_count):
    matches = lookup_keys[..., None] == jnp.arange(entry_count, dtype=jnp.int32)
    return jnp.sum(jnp.where(matches, lookup_table, 0), axis=-1)


def widen(pieces, half_count):
    return jnp.tile(pieces, (half_count,) + (1,) * (pieces.ndim - 1))


def pair_halves(upper_half, own_rows, other_rows):
    return jnp.where(
        upper_half,
        jnp.stack([other_rows, own_rows], axis=1),
        jnp.stack([own_rows, other_rows], axis=1),
    )


def local(tokens, router_probs, expert_ids, old_place, new_place, w_gate, w_up, w_down):
    slot_count = old_place.shape[0]
    tok_count, top_count = expert_ids.shape
    model_width = tokens.shape[1]
    n_shard = lax.axis_size("shard")
    half_count = n_shard // 2
    column = lax.axis_index("shard")
    row_id = lax.axis_index("dp")
    n_rows = lax.axis_size("dp")
    upper_half = column % 2 == 1
    capacity = max(2, 2 * tok_count * top_count // slot_count)
    places = slot_count * capacity
    stacked = jnp.stack([w_gate, w_up, w_down], axis=1)
    full = lax.all_to_all(widen(stacked, half_count), "shard", split_axis=0, concat_axis=2, tiled=True)
    full_gate = full[0, 0]
    full_up = full[0, 1]
    full_down = full[0, 2]
    slot_index = jnp.arange(slot_count, dtype=jnp.int32)
    owner_slot = jnp.sum(
        jnp.where(old_place[None, :] == slot_index[:, None], slot_index[None, :], 0), axis=1
    )
    slot_ids = lookup(expert_ids, owner_slot, slot_count)
    gate_weights = (router_probs / jnp.sum(router_probs, axis=1, keepdims=True)).astype(
        jnp.bfloat16
    )
    side = jnp.concatenate(
        [
            slot_ids.astype(jnp.bfloat16),
            jnp.zeros((tok_count, 128 - top_count), jnp.bfloat16),
        ],
        axis=1,
    )
    gathered = lax.all_gather(jnp.concatenate([tokens, side], axis=1), "dp", axis=0, tiled=False)
    gathered_tokens = gathered[..., :model_width]
    gathered_slots = (
        gathered[..., model_width : model_width + top_count].astype(jnp.int32).reshape(n_rows, -1)
    )
    row_slots = 2 * row_id + jnp.arange(2, dtype=jnp.int32)
    in_row = (gathered_slots[:, :, None] == row_slots[None, None, :]).astype(jnp.int32)
    row_rank = jnp.cumsum(in_row, axis=1) - in_row
    picks = (in_row[..., None] == 1) & (
        row_rank[..., None] == jnp.arange(capacity, dtype=jnp.int32)
    )
    picks = picks.reshape(n_rows, tok_count, top_count, 2, capacity)
    picks = jnp.any(picks, axis=2)
    arrived = jnp.einsum(
        "stcr,std->scrd",
        picks.astype(jnp.bfloat16),
        gathered_tokens,
        preferred_element_type=jnp.float32,
    ).astype(jnp.bfloat16)
    own_rows = jnp.where(upper_half, arrived[:, 1], arrived[:, 0])
    other_rows = jnp.where(upper_half, arrived[:, 0], arrived[:, 1])
    partner = partner_2(other_rows, "shard", 0)
    work_rows = jnp.stack([own_rows, partner], axis=0)
    flat_rows = work_rows.reshape(-1, model_width)
    gate_part = jnp.dot(flat_rows, full_gate, preferred_element_type=jnp.float32)
    up_part = jnp.dot(flat_rows, full_up, preferred_element_type=jnp.float32)
    hidden = (jax.nn.silu(gate_part) * up_part).astype(jnp.bfloat16)
    result = lax.dot_general(
        hidden, full_down, (((1,), (1,)), ((), ())), preferred_element_type=jnp.float32
    ).astype(jnp.bfloat16)
    result = result.reshape(2, n_rows, capacity, model_width)
    returned_other = partner_2(result[1], "shard", 0)
    returned = lax.all_to_all(
        pair_halves(upper_half, result[0], returned_other),
        "dp",
        split_axis=0,
        concat_axis=0,
        tiled=True,
    )
    flat_slots = slot_ids.reshape(-1)
    members = (flat_slots[:, None] == slot_index[None, :]).astype(jnp.int32)
    earlier = jnp.cumsum(members, axis=0) - members
    slot_rank = jnp.sum(earlier * members, axis=1)
    position = (flat_slots * capacity + slot_rank).reshape(tok_count, top_count)
    matches = position[:, :, None] == jnp.arange(places, dtype=jnp.int32)[None, None, :]
    combine = jnp.sum(
        jnp.where(matches, gate_weights[:, :, None], jnp.zeros((), jnp.bfloat16)), axis=1
    )
    moe_output = jnp.dot(
        combine, returned.reshape(places, model_width), preferred_element_type=jnp.float32
    ).astype(jnp.bfloat16)
    base_slot = 2 * row_id
    second_old = lax.dynamic_index_in_dim(old_place, base_slot + 1, 0, keepdims=False)
    second_new = lax.dynamic_index_in_dim(new_place, base_slot + 1, 0, keepdims=False)
    second_moved = second_new != second_old
    leave_gate = jnp.where(second_moved, w_gate[1], w_gate[0])
    leave_up = jnp.where(second_moved, w_up[1], w_up[0])
    leave_down = jnp.where(second_moved, w_down[1], w_down[0])
    arrive_gate, arrive_up, arrive_down = passed_along((leave_gate, leave_up, leave_down), "dp", 1)
    new_gate = jnp.stack(
        [
            jnp.where(second_moved, w_gate[0], arrive_gate),
            jnp.where(second_moved, arrive_gate, w_gate[1]),
        ],
        axis=0,
    )
    new_up = jnp.stack(
        [jnp.where(second_moved, w_up[0], arrive_up), jnp.where(second_moved, arrive_up, w_up[1])],
        axis=0,
    )
    new_down = jnp.stack(
        [
            jnp.where(second_moved, w_down[0], arrive_down),
            jnp.where(second_moved, arrive_down, w_down[1]),
        ],
        axis=0,
    )
    return (moe_output, new_gate, new_up, new_down)


def solution(mesh):
    in_specs = (
        P(("dp", "shard"), None),
        P(("dp", "shard"), None),
        P(("dp", "shard"), None),
        P(),
        P(),
        P("dp", "shard", None),
        P("dp", "shard", None),
        P("dp", "shard", None),
    )
    out_specs = (
        P(("dp", "shard"), None),
        P("dp", "shard", None),
        P("dp", "shard", None),
        P("dp", "shard", None),
    )
    return jax.shard_map(local, mesh=mesh, in_specs=in_specs, out_specs=out_specs, check_vma=False)
```

```python
import jax
import jax.numpy as jnp
from jax import lax
from jax.experimental import pallas as pl
from jax.experimental.pallas import tpu as pltpu
from jax.sharding import PartitionSpec as P


def gather_kernel(n_shard, *refs):
    sources, outputs = refs[0:3], refs[3:6]
    send_sem, recv_sem, local_sem = refs[6:9]
    me = lax.axis_index("shard")
    row = lax.axis_index("dp")

    def remote(w, peer, sender, target):
        return pltpu.make_async_remote_copy(
            src_ref=sources[w].at[peer % 2],
            dst_ref=outputs[w].at[sender],
            send_sem=send_sem.at[w, peer],
            recv_sem=recv_sem.at[w, sender],
            device_id=(row, target),
            device_id_type=pl.DeviceIdType.MESH,
        )

    def local(w):
        return pltpu.make_async_copy(
            sources[w].at[me % 2], outputs[w].at[me], local_sem.at[w]
        )

    for w in range(3):
        for peer in range(n_shard):

            @pl.when(peer != me)
            def _():
                remote(w, peer, me, peer).start()

        local(w).start()
    for w in range(3):
        local(w).wait()
        for peer in range(n_shard):

            @pl.when(peer != me)
            def _():
                remote(w, peer, me, peer).wait_send()
                remote(w, peer, peer, peer).wait_recv()


def gather_slots(w_gate, w_up, w_down, n_shard):
    piece = jax.ShapeDtypeStruct((n_shard,) + w_gate.shape[1:], w_gate.dtype)
    anywhere = pl.BlockSpec(memory_space=pl.ANY)
    return pl.pallas_call(
        lambda *refs: gather_kernel(n_shard, *refs),
        out_shape=(piece, piece, piece),
        in_specs=[anywhere] * 3,
        out_specs=(anywhere, anywhere, anywhere),
        scratch_shapes=[
            pltpu.SemaphoreType.DMA((3, n_shard)),
            pltpu.SemaphoreType.DMA((3, n_shard)),
            pltpu.SemaphoreType.DMA((3,)),
        ],
        compiler_params=pltpu.CompilerParams(has_side_effects=True),
        cost_estimate=pl.CostEstimate(
            flops=0, bytes_accessed=6 * n_shard * w_gate[0].size * 2, transcendentals=0
        ),
    )(w_gate, w_up, w_down)


def partner_2(x, axis, apart):
    return lax.ppermute(x, axis, [(i, i ^ 1 << apart) for i in range(lax.axis_size(axis))])


def passed_along(x, axis, by):
    size = lax.axis_size(axis)
    return lax.ppermute(x, axis, [(i, (i + by) % size) for i in range(size)])


def lookup(lookup_keys, lookup_table, entry_count):
    matches = lookup_keys[..., None] == jnp.arange(entry_count, dtype=jnp.int32)
    return jnp.sum(jnp.where(matches, lookup_table, 0), axis=-1)


def widen(pieces, half_count):
    return jnp.tile(pieces, (half_count, 1, 1))


def pair_halves(upper_half, own_rows, other_rows):
    return jnp.where(
        upper_half,
        jnp.stack([other_rows, own_rows], axis=1),
        jnp.stack([own_rows, other_rows], axis=1),
    )


def local(tokens, router_probs, expert_ids, old_place, new_place, w_gate, w_up, w_down):
    slot_count = old_place.shape[0]
    tok_count, top_count = expert_ids.shape
    model_width = tokens.shape[1]
    n_shard = lax.axis_size("shard")
    half_count = n_shard // 2
    column = lax.axis_index("shard")
    row_id = lax.axis_index("dp")
    n_rows = lax.axis_size("dp")
    upper_half = column % 2 == 1
    capacity = max(2, 2 * tok_count * top_count // slot_count)
    places = slot_count * capacity
    slot_index = jnp.arange(slot_count, dtype=jnp.int32)
    owner_slot = jnp.sum(
        jnp.where(old_place[None, :] == slot_index[:, None], slot_index[None, :], 0), axis=1
    )
    slot_ids = lookup(expert_ids, owner_slot, slot_count)
    gate_weights = (router_probs / jnp.sum(router_probs, axis=1, keepdims=True)).astype(
        jnp.bfloat16
    )
    side = jnp.concatenate(
        [
            slot_ids.astype(jnp.bfloat16),
            jnp.zeros((tok_count, 128 - top_count), jnp.bfloat16),
        ],
        axis=1,
    )
    gathered = lax.all_gather(jnp.concatenate([tokens, side], axis=1), "dp", axis=0, tiled=False)
    full_slots = gather_slots(w_gate, w_up, w_down, n_shard)
    gathered, full_slots = lax.optimization_barrier((gathered, full_slots))
    full_gate, full_up, full_down = (piece.reshape(model_width, -1) for piece in full_slots)
    gathered_tokens = gathered[..., :model_width]
    gathered_slots = (
        gathered[..., model_width : model_width + top_count].astype(jnp.int32).reshape(n_rows, -1)
    )
    row_slots = 2 * row_id + jnp.arange(2, dtype=jnp.int32)
    in_row = (gathered_slots[:, :, None] == row_slots[None, None, :]).astype(jnp.int32)
    row_rank = jnp.cumsum(in_row, axis=1) - in_row
    picks = (in_row[..., None] == 1) & (
        row_rank[..., None] == jnp.arange(capacity, dtype=jnp.int32)
    )
    picks = picks.reshape(n_rows, tok_count, top_count, 2, capacity)
    picks = jnp.any(picks, axis=2)
    arrived = jnp.einsum(
        "stcr,std->scrd",
        picks.astype(jnp.bfloat16),
        gathered_tokens,
        preferred_element_type=jnp.float32,
    ).astype(jnp.bfloat16)
    own_rows = jnp.where(upper_half, arrived[:, 1], arrived[:, 0])
    other_rows = jnp.where(upper_half, arrived[:, 0], arrived[:, 1])
    partner = partner_2(other_rows, "shard", 0)
    work_rows = jnp.stack([own_rows, partner], axis=0)
    flat_rows = work_rows.reshape(-1, model_width)
    gate_part = jnp.dot(flat_rows, full_gate, preferred_element_type=jnp.float32)
    up_part = jnp.dot(flat_rows, full_up, preferred_element_type=jnp.float32)
    hidden = (jax.nn.silu(gate_part) * up_part).astype(jnp.bfloat16)
    result = lax.dot_general(
        hidden, full_down, (((1,), (1,)), ((), ())), preferred_element_type=jnp.float32
    ).astype(jnp.bfloat16)
    result = result.reshape(2, n_rows, capacity, model_width)
    returned_other = partner_2(result[1], "shard", 0)
    returned = lax.all_to_all(
        pair_halves(upper_half, result[0], returned_other),
        "dp",
        split_axis=0,
        concat_axis=0,
        tiled=True,
    )
    flat_slots = slot_ids.reshape(-1)
    members = (flat_slots[:, None] == slot_index[None, :]).astype(jnp.int32)
    earlier = jnp.cumsum(members, axis=0) - members
    slot_rank = jnp.sum(earlier * members, axis=1)
    position = (flat_slots * capacity + slot_rank).reshape(tok_count, top_count)
    matches = position[:, :, None] == jnp.arange(places, dtype=jnp.int32)[None, None, :]
    combine = jnp.sum(
        jnp.where(matches, gate_weights[:, :, None], jnp.zeros((), jnp.bfloat16)), axis=1
    )
    moe_output = jnp.dot(
        combine, returned.reshape(places, model_width), preferred_element_type=jnp.float32
    ).astype(jnp.bfloat16)
    base_slot = 2 * row_id
    second_old = lax.dynamic_index_in_dim(old_place, base_slot + 1, 0, keepdims=False)
    second_new = lax.dynamic_index_in_dim(new_place, base_slot + 1, 0, keepdims=False)
    second_moved = second_new != second_old
    leave_gate = jnp.where(second_moved, w_gate[1], w_gate[0])
    leave_up = jnp.where(second_moved, w_up[1], w_up[0])
    leave_down = jnp.where(second_moved, w_down[1], w_down[0])
    arrive_gate, arrive_up, arrive_down = passed_along((leave_gate, leave_up, leave_down), "dp", 1)
    new_gate = jnp.stack(
        [
            jnp.where(second_moved, w_gate[0], arrive_gate),
            jnp.where(second_moved, arrive_gate, w_gate[1]),
        ],
        axis=0,
    )
    new_up = jnp.stack(
        [jnp.where(second_moved, w_up[0], arrive_up), jnp.where(second_moved, arrive_up, w_up[1])],
        axis=0,
    )
    new_down = jnp.stack(
        [
            jnp.where(second_moved, w_down[0], arrive_down),
            jnp.where(second_moved, arrive_down, w_down[1]),
        ],
        axis=0,
    )
    return (moe_output, new_gate, new_up, new_down)


def solution(mesh):
    in_specs = (
        P(("dp", "shard"), None),
        P(("dp", "shard"), None),
        P(("dp", "shard"), None),
        P(),
        P(),
        P("dp", "shard", None),
        P("dp", "shard", None),
        P("dp", "shard", None),
    )
    out_specs = (
        P(("dp", "shard"), None),
        P("dp", "shard", None),
        P("dp", "shard", None),
        P("dp", "shard", None),
    )
    return jax.shard_map(local, mesh=mesh, in_specs=in_specs, out_specs=out_specs, check_vma=False)
```

```python
import jax
import jax.numpy as jnp
from jax import lax
from jax.sharding import PartitionSpec as P


def partner_2(x, axis, apart):
    return lax.ppermute(x, axis, [(i, i ^ 1 << apart) for i in range(lax.axis_size(axis))])


def passed_along(x, axis, by):
    size = lax.axis_size(axis)
    return lax.ppermute(x, axis, [(i, (i + by) % size) for i in range(size)])


def lookup(lookup_keys, lookup_table, entry_count):
    matches = lookup_keys[..., None] == jnp.arange(entry_count, dtype=jnp.int32)
    return jnp.sum(jnp.where(matches, lookup_table, 0), axis=-1)


def widen(pieces, half_count):
    return jnp.tile(pieces, (half_count, 1, 1))


def pair_halves(upper_half, own_rows, other_rows):
    return jnp.where(
        upper_half,
        jnp.stack([other_rows, own_rows], axis=1),
        jnp.stack([own_rows, other_rows], axis=1),
    )


def local(tokens, router_probs, expert_ids, old_place, new_place, w_gate, w_up, w_down):
    slot_count = old_place.shape[0]
    tok_count, top_count = expert_ids.shape
    model_width = tokens.shape[1]
    n_shard = lax.axis_size("shard")
    half_count = n_shard // 2
    column = lax.axis_index("shard")
    row_id = lax.axis_index("dp")
    n_rows = lax.axis_size("dp")
    upper_half = column % 2 == 1
    capacity = max(2, 2 * tok_count * top_count // slot_count)
    places = slot_count * capacity
    full_gate, full_up, full_down = (
        lax.all_to_all(widen(w_gate, half_count), "shard", split_axis=0, concat_axis=1, tiled=True),
        lax.all_to_all(widen(w_up, half_count), "shard", split_axis=0, concat_axis=1, tiled=True),
        lax.all_to_all(widen(w_down, half_count), "shard", split_axis=0, concat_axis=1, tiled=True),
    )
    full_gate = full_gate[0]
    full_up = full_up[0]
    full_down = full_down[0]
    slot_index = jnp.arange(slot_count, dtype=jnp.int32)
    owner_slot = jnp.sum(
        jnp.where(old_place[None, :] == slot_index[:, None], slot_index[None, :], 0), axis=1
    )
    slot_ids = lookup(expert_ids, owner_slot, slot_count)
    gate_weights = (router_probs / jnp.sum(router_probs, axis=1, keepdims=True)).astype(
        jnp.bfloat16
    )
    side = jnp.concatenate(
        [
            slot_ids.astype(jnp.bfloat16),
            jnp.zeros((tok_count, 128 - top_count), jnp.bfloat16),
        ],
        axis=1,
    )
    ext = jnp.concatenate([tokens, side], axis=1)
    pair = jnp.stack([ext, partner_2(ext, "dp", 0)], axis=0)
    pair = jnp.where(row_id % 2 == 1, pair[::-1], pair)
    groups = [list(range(g, n_rows, 2)) for g in range(2)]
    gathered = lax.all_gather(pair, "dp", axis=0, tiled=True, axis_index_groups=groups)
    gathered = gathered.reshape(n_rows, tok_count, -1)
    gathered_tokens = gathered[..., :model_width]
    gathered_slots = (
        gathered[..., model_width : model_width + top_count].astype(jnp.int32).reshape(n_rows, -1)
    )
    row_slots = 2 * row_id + jnp.arange(2, dtype=jnp.int32)
    in_row = (gathered_slots[:, :, None] == row_slots[None, None, :]).astype(jnp.int32)
    row_rank = jnp.cumsum(in_row, axis=1) - in_row
    picks = (in_row[..., None] == 1) & (
        row_rank[..., None] == jnp.arange(capacity, dtype=jnp.int32)
    )
    picks = picks.reshape(n_rows, tok_count, top_count, 2, capacity)
    picks = jnp.any(picks, axis=2)
    arrived = jnp.einsum(
        "stcr,std->scrd",
        picks.astype(jnp.bfloat16),
        gathered_tokens,
        preferred_element_type=jnp.float32,
    ).astype(jnp.bfloat16)
    own_rows = jnp.where(upper_half, arrived[:, 1], arrived[:, 0])
    other_rows = jnp.where(upper_half, arrived[:, 0], arrived[:, 1])
    partner = partner_2(other_rows, "shard", 0)
    work_rows = jnp.stack([own_rows, partner], axis=0)
    flat_rows = work_rows.reshape(-1, model_width)
    gate_part = jnp.dot(flat_rows, full_gate, preferred_element_type=jnp.float32)
    up_part = jnp.dot(flat_rows, full_up, preferred_element_type=jnp.float32)
    hidden = (jax.nn.silu(gate_part) * up_part).astype(jnp.bfloat16)
    result = lax.dot_general(
        hidden, full_down, (((1,), (1,)), ((), ())), preferred_element_type=jnp.float32
    ).astype(jnp.bfloat16)
    result = result.reshape(2, n_rows, capacity, model_width)
    returned_other = partner_2(result[1], "shard", 0)
    returned = lax.all_to_all(
        pair_halves(upper_half, result[0], returned_other),
        "dp",
        split_axis=0,
        concat_axis=0,
        tiled=True,
    )
    flat_slots = slot_ids.reshape(-1)
    members = (flat_slots[:, None] == slot_index[None, :]).astype(jnp.int32)
    earlier = jnp.cumsum(members, axis=0) - members
    slot_rank = jnp.sum(earlier * members, axis=1)
    position = (flat_slots * capacity + slot_rank).reshape(tok_count, top_count)
    matches = position[:, :, None] == jnp.arange(places, dtype=jnp.int32)[None, None, :]
    combine = jnp.sum(
        jnp.where(matches, gate_weights[:, :, None], jnp.zeros((), jnp.bfloat16)), axis=1
    )
    moe_output = jnp.dot(
        combine, returned.reshape(places, model_width), preferred_element_type=jnp.float32
    ).astype(jnp.bfloat16)
    base_slot = 2 * row_id
    second_old = lax.dynamic_index_in_dim(old_place, base_slot + 1, 0, keepdims=False)
    second_new = lax.dynamic_index_in_dim(new_place, base_slot + 1, 0, keepdims=False)
    second_moved = second_new != second_old
    leave_gate = jnp.where(second_moved, w_gate[1], w_gate[0])
    leave_up = jnp.where(second_moved, w_up[1], w_up[0])
    leave_down = jnp.where(second_moved, w_down[1], w_down[0])
    arrive_gate, arrive_up, arrive_down = passed_along((leave_gate, leave_up, leave_down), "dp", 1)
    new_gate = jnp.stack(
        [
            jnp.where(second_moved, w_gate[0], arrive_gate),
            jnp.where(second_moved, arrive_gate, w_gate[1]),
        ],
        axis=0,
    )
    new_up = jnp.stack(
        [jnp.where(second_moved, w_up[0], arrive_up), jnp.where(second_moved, arrive_up, w_up[1])],
        axis=0,
    )
    new_down = jnp.stack(
        [
            jnp.where(second_moved, w_down[0], arrive_down),
            jnp.where(second_moved, arrive_down, w_down[1]),
        ],
        axis=0,
    )
    return (moe_output, new_gate, new_up, new_down)


def solution(mesh):
    in_specs = (
        P(("dp", "shard"), None),
        P(("dp", "shard"), None),
        P(("dp", "shard"), None),
        P(),
        P(),
        P("dp", "shard", None),
        P("dp", "shard", None),
        P("dp", "shard", None),
    )
    out_specs = (
        P(("dp", "shard"), None),
        P("dp", "shard", None),
        P("dp", "shard", None),
        P("dp", "shard", None),
    )
    return jax.shard_map(local, mesh=mesh, in_specs=in_specs, out_specs=out_specs, check_vma=False)
```

```python
import jax
import jax.numpy as jnp
from jax import lax
from jax.experimental import pallas as pl
from jax.experimental.pallas import tpu as pltpu
from jax.sharding import PartitionSpec as P


def gather_kernel(n_shard, *refs):
    sources, outputs = refs[0:3], refs[3:6]
    send_sem, recv_sem, local_sem = refs[6:9]
    me = lax.axis_index("shard")
    row = lax.axis_index("dp")

    def remote(w, peer, sender, target):
        return pltpu.make_async_remote_copy(
            src_ref=sources[w].at[peer % 2],
            dst_ref=outputs[w].at[sender],
            send_sem=send_sem.at[w, peer],
            recv_sem=recv_sem.at[w, sender],
            device_id=(row, target),
            device_id_type=pl.DeviceIdType.MESH,
        )

    def local(w):
        return pltpu.make_async_copy(
            sources[w].at[me % 2], outputs[w].at[me], local_sem.at[w]
        )

    for w in range(3):
        for peer in range(n_shard):

            @pl.when(peer != me)
            def _():
                remote(w, peer, me, peer).start()

        local(w).start()
    for w in range(3):
        local(w).wait()
        for peer in range(n_shard):

            @pl.when(peer != me)
            def _():
                remote(w, peer, me, peer).wait_send()
                remote(w, peer, peer, peer).wait_recv()


def gather_slots(w_gate, w_up, w_down, n_shard):
    piece = jax.ShapeDtypeStruct((n_shard,) + w_gate.shape[1:], w_gate.dtype)
    anywhere = pl.BlockSpec(memory_space=pl.ANY)
    return pl.pallas_call(
        lambda *refs: gather_kernel(n_shard, *refs),
        out_shape=(piece, piece, piece),
        in_specs=[anywhere] * 3,
        out_specs=(anywhere, anywhere, anywhere),
        scratch_shapes=[
            pltpu.SemaphoreType.DMA((3, n_shard)),
            pltpu.SemaphoreType.DMA((3, n_shard)),
            pltpu.SemaphoreType.DMA((3,)),
        ],
        compiler_params=pltpu.CompilerParams(has_side_effects=True),
        cost_estimate=pl.CostEstimate(
            flops=0, bytes_accessed=6 * n_shard * w_gate[0].size * 2, transcendentals=0
        ),
    )(w_gate, w_up, w_down)


def partner_2(x, axis, apart):
    return lax.ppermute(x, axis, [(i, i ^ 1 << apart) for i in range(lax.axis_size(axis))])


def passed_along(x, axis, by):
    size = lax.axis_size(axis)
    return lax.ppermute(x, axis, [(i, (i + by) % size) for i in range(size)])


def lookup(lookup_keys, lookup_table, entry_count):
    matches = lookup_keys[..., None] == jnp.arange(entry_count, dtype=jnp.int32)
    return jnp.sum(jnp.where(matches, lookup_table, 0), axis=-1)


def widen(pieces, half_count):
    return jnp.tile(pieces, (half_count, 1, 1))


def pair_halves(upper_half, own_rows, other_rows):
    return jnp.where(
        upper_half,
        jnp.stack([other_rows, own_rows], axis=1),
        jnp.stack([own_rows, other_rows], axis=1),
    )


def local(tokens, router_probs, expert_ids, old_place, new_place, w_gate, w_up, w_down):
    slot_count = old_place.shape[0]
    tok_count, top_count = expert_ids.shape
    model_width = tokens.shape[1]
    n_shard = lax.axis_size("shard")
    half_count = n_shard // 2
    column = lax.axis_index("shard")
    row_id = lax.axis_index("dp")
    n_rows = lax.axis_size("dp")
    upper_half = column % 2 == 1
    capacity = max(2, 2 * tok_count * top_count // slot_count)
    places = slot_count * capacity
    slot_index = jnp.arange(slot_count, dtype=jnp.int32)
    owner_slot = jnp.sum(
        jnp.where(old_place[None, :] == slot_index[:, None], slot_index[None, :], 0), axis=1
    )
    slot_ids = lookup(expert_ids, owner_slot, slot_count)
    gate_weights = (router_probs / jnp.sum(router_probs, axis=1, keepdims=True)).astype(
        jnp.bfloat16
    )
    side = jnp.concatenate(
        [
            slot_ids.astype(jnp.bfloat16),
            jnp.zeros((tok_count, 128 - top_count), jnp.bfloat16),
        ],
        axis=1,
    )
    ext = jnp.concatenate([tokens, side], axis=1)
    pair = jnp.stack([ext, partner_2(ext, "dp", 0)], axis=0)
    pair = jnp.where(row_id % 2 == 1, pair[::-1], pair)
    groups = [list(range(g, n_rows, 2)) for g in range(2)]
    gathered = lax.all_gather(pair, "dp", axis=0, tiled=True, axis_index_groups=groups)
    gathered = gathered.reshape(n_rows, tok_count, -1)
    full_slots = gather_slots(w_gate, w_up, w_down, n_shard)
    gathered, full_slots = lax.optimization_barrier((gathered, full_slots))
    full_gate, full_up, full_down = (piece.reshape(model_width, -1) for piece in full_slots)
    gathered_tokens = gathered[..., :model_width]
    gathered_slots = (
        gathered[..., model_width : model_width + top_count].astype(jnp.int32).reshape(n_rows, -1)
    )
    row_slots = 2 * row_id + jnp.arange(2, dtype=jnp.int32)
    in_row = (gathered_slots[:, :, None] == row_slots[None, None, :]).astype(jnp.int32)
    row_rank = jnp.cumsum(in_row, axis=1) - in_row
    picks = (in_row[..., None] == 1) & (
        row_rank[..., None] == jnp.arange(capacity, dtype=jnp.int32)
    )
    picks = picks.reshape(n_rows, tok_count, top_count, 2, capacity)
    picks = jnp.any(picks, axis=2)
    arrived = jnp.einsum(
        "stcr,std->scrd",
        picks.astype(jnp.bfloat16),
        gathered_tokens,
        preferred_element_type=jnp.float32,
    ).astype(jnp.bfloat16)
    own_rows = jnp.where(upper_half, arrived[:, 1], arrived[:, 0])
    other_rows = jnp.where(upper_half, arrived[:, 0], arrived[:, 1])
    partner = partner_2(other_rows, "shard", 0)
    work_rows = jnp.stack([own_rows, partner], axis=0)
    flat_rows = work_rows.reshape(-1, model_width)
    gate_part = jnp.dot(flat_rows, full_gate, preferred_element_type=jnp.float32)
    up_part = jnp.dot(flat_rows, full_up, preferred_element_type=jnp.float32)
    hidden = (jax.nn.silu(gate_part) * up_part).astype(jnp.bfloat16)
    result = lax.dot_general(
        hidden, full_down, (((1,), (1,)), ((), ())), preferred_element_type=jnp.float32
    ).astype(jnp.bfloat16)
    result = result.reshape(2, n_rows, capacity, model_width)
    returned_other = partner_2(result[1], "shard", 0)
    returned = lax.all_to_all(
        pair_halves(upper_half, result[0], returned_other),
        "dp",
        split_axis=0,
        concat_axis=0,
        tiled=True,
    )
    flat_slots = slot_ids.reshape(-1)
    members = (flat_slots[:, None] == slot_index[None, :]).astype(jnp.int32)
    earlier = jnp.cumsum(members, axis=0) - members
    slot_rank = jnp.sum(earlier * members, axis=1)
    position = (flat_slots * capacity + slot_rank).reshape(tok_count, top_count)
    matches = position[:, :, None] == jnp.arange(places, dtype=jnp.int32)[None, None, :]
    combine = jnp.sum(
        jnp.where(matches, gate_weights[:, :, None], jnp.zeros((), jnp.bfloat16)), axis=1
    )
    moe_output = jnp.dot(
        combine, returned.reshape(places, model_width), preferred_element_type=jnp.float32
    ).astype(jnp.bfloat16)
    base_slot = 2 * row_id
    second_old = lax.dynamic_index_in_dim(old_place, base_slot + 1, 0, keepdims=False)
    second_new = lax.dynamic_index_in_dim(new_place, base_slot + 1, 0, keepdims=False)
    second_moved = second_new != second_old
    leave_gate = jnp.where(second_moved, w_gate[1], w_gate[0])
    leave_up = jnp.where(second_moved, w_up[1], w_up[0])
    leave_down = jnp.where(second_moved, w_down[1], w_down[0])
    arrive_gate, arrive_up, arrive_down = passed_along((leave_gate, leave_up, leave_down), "dp", 1)
    new_gate = jnp.stack(
        [
            jnp.where(second_moved, w_gate[0], arrive_gate),
            jnp.where(second_moved, arrive_gate, w_gate[1]),
        ],
        axis=0,
    )
    new_up = jnp.stack(
        [jnp.where(second_moved, w_up[0], arrive_up), jnp.where(second_moved, arrive_up, w_up[1])],
        axis=0,
    )
    new_down = jnp.stack(
        [
            jnp.where(second_moved, w_down[0], arrive_down),
            jnp.where(second_moved, arrive_down, w_down[1]),
        ],
        axis=0,
    )
    return (moe_output, new_gate, new_up, new_down)


def solution(mesh):
    in_specs = (
        P(("dp", "shard"), None),
        P(("dp", "shard"), None),
        P(("dp", "shard"), None),
        P(),
        P(),
        P("dp", "shard", None),
        P("dp", "shard", None),
        P("dp", "shard", None),
    )
    out_specs = (
        P(("dp", "shard"), None),
        P("dp", "shard", None),
        P("dp", "shard", None),
        P("dp", "shard", None),
    )
    return jax.shard_map(local, mesh=mesh, in_specs=in_specs, out_specs=out_specs, check_vma=False)
```

```python
import jax
import jax.numpy as jnp
from jax import lax
from jax.sharding import PartitionSpec as P


def partner_2(x, axis, apart):
    return lax.ppermute(x, axis, [(i, i ^ 1 << apart) for i in range(lax.axis_size(axis))])


def passed_along(x, axis, by):
    size = lax.axis_size(axis)
    return lax.ppermute(x, axis, [(i, (i + by) % size) for i in range(size)])


def lookup(lookup_keys, lookup_table, entry_count):
    matches = lookup_keys[..., None] == jnp.arange(entry_count, dtype=jnp.int32)
    return jnp.sum(jnp.where(matches, lookup_table, 0), axis=-1)


def widen(pieces, half_count):
    return jnp.tile(pieces, (half_count, 1, 1))


def pair_halves(upper_half, own_rows, other_rows):
    return jnp.where(
        upper_half,
        jnp.stack([other_rows, own_rows], axis=1),
        jnp.stack([own_rows, other_rows], axis=1),
    )


def local(tokens, router_probs, expert_ids, old_place, new_place, w_gate, w_up, w_down):
    slot_count = old_place.shape[0]
    tok_count, top_count = expert_ids.shape
    model_width = tokens.shape[1]
    n_shard = lax.axis_size("shard")
    half_count = n_shard // 2
    column = lax.axis_index("shard")
    row_id = lax.axis_index("dp")
    n_rows = lax.axis_size("dp")
    upper_half = column % 2 == 1
    capacity = max(2, 2 * tok_count * top_count // slot_count)
    places = slot_count * capacity
    full_gate, full_up, full_down = (
        lax.all_to_all(widen(w_gate, half_count), "shard", split_axis=0, concat_axis=1, tiled=True),
        lax.all_to_all(widen(w_up, half_count), "shard", split_axis=0, concat_axis=1, tiled=True),
        lax.all_to_all(widen(w_down, half_count), "shard", split_axis=0, concat_axis=1, tiled=True),
    )
    full_gate = full_gate[0]
    full_up = full_up[0]
    full_down = full_down[0]
    slot_index = jnp.arange(slot_count, dtype=jnp.int32)
    owner_slot = jnp.sum(
        jnp.where(old_place[None, :] == slot_index[:, None], slot_index[None, :], 0), axis=1
    )
    slot_ids = lookup(expert_ids, owner_slot, slot_count)
    gate_weights = (router_probs / jnp.sum(router_probs, axis=1, keepdims=True)).astype(
        jnp.bfloat16
    )
    side = jnp.concatenate(
        [
            slot_ids.astype(jnp.bfloat16),
            jnp.zeros((tok_count, 128 - top_count), jnp.bfloat16),
        ],
        axis=1,
    )
    ext = jnp.concatenate([tokens, side], axis=1)
    pair = jnp.stack([ext, partner_2(ext, "dp", 0)], axis=0)
    pair = jnp.where(row_id % 2 == 1, pair[::-1], pair)
    groups = [list(range(g, n_rows, 2)) for g in range(2)]
    gathered = lax.all_gather(pair, "dp", axis=0, tiled=True, axis_index_groups=groups)
    gathered = gathered.reshape(n_rows, tok_count, -1)
    gathered_tokens = gathered[..., :model_width]
    gathered_slots = (
        gathered[..., model_width : model_width + top_count].astype(jnp.int32).reshape(n_rows, -1)
    )
    row_slots = 2 * row_id + jnp.arange(2, dtype=jnp.int32)
    in_row = (gathered_slots[:, :, None] == row_slots[None, None, :]).astype(jnp.int32)
    row_rank = jnp.cumsum(in_row, axis=1) - in_row
    picks = (in_row[..., None] == 1) & (
        row_rank[..., None] == jnp.arange(capacity, dtype=jnp.int32)
    )
    picks = picks.reshape(n_rows, tok_count, top_count, 2, capacity)
    picks = jnp.any(picks, axis=2)
    arrived = jnp.einsum(
        "stcr,std->scrd",
        picks.astype(jnp.bfloat16),
        gathered_tokens,
        preferred_element_type=jnp.float32,
    ).astype(jnp.bfloat16)
    own_rows = jnp.where(upper_half, arrived[:, 1], arrived[:, 0])
    other_rows = jnp.where(upper_half, arrived[:, 0], arrived[:, 1])
    partner = partner_2(other_rows, "shard", 0)
    work_rows = jnp.stack([own_rows, partner], axis=0)
    base_slot = 2 * row_id
    second_old = lax.dynamic_index_in_dim(old_place, base_slot + 1, 0, keepdims=False)
    second_new = lax.dynamic_index_in_dim(new_place, base_slot + 1, 0, keepdims=False)
    second_moved = second_new != second_old
    leave_gate = jnp.where(second_moved, w_gate[1], w_gate[0])
    leave_up = jnp.where(second_moved, w_up[1], w_up[0])
    leave_down = jnp.where(second_moved, w_down[1], w_down[0])
    arrive_gate, arrive_up, arrive_down = passed_along((leave_gate, leave_up, leave_down), "dp", 1)
    work_rows, arrive_gate, arrive_up, arrive_down = lax.optimization_barrier(
        (work_rows, arrive_gate, arrive_up, arrive_down)
    )
    flat_rows = work_rows.reshape(-1, model_width)
    gate_part = jnp.dot(flat_rows, full_gate, preferred_element_type=jnp.float32)
    up_part = jnp.dot(flat_rows, full_up, preferred_element_type=jnp.float32)
    hidden = (jax.nn.silu(gate_part) * up_part).astype(jnp.bfloat16)
    result = lax.dot_general(
        hidden, full_down, (((1,), (1,)), ((), ())), preferred_element_type=jnp.float32
    ).astype(jnp.bfloat16)
    result = result.reshape(2, n_rows, capacity, model_width)
    returned_other = partner_2(result[1], "shard", 0)
    returned = lax.all_to_all(
        pair_halves(upper_half, result[0], returned_other),
        "dp",
        split_axis=0,
        concat_axis=0,
        tiled=True,
    )
    flat_slots = slot_ids.reshape(-1)
    members = (flat_slots[:, None] == slot_index[None, :]).astype(jnp.int32)
    earlier = jnp.cumsum(members, axis=0) - members
    slot_rank = jnp.sum(earlier * members, axis=1)
    position = (flat_slots * capacity + slot_rank).reshape(tok_count, top_count)
    matches = position[:, :, None] == jnp.arange(places, dtype=jnp.int32)[None, None, :]
    combine = jnp.sum(
        jnp.where(matches, gate_weights[:, :, None], jnp.zeros((), jnp.bfloat16)), axis=1
    )
    moe_output = jnp.dot(
        combine, returned.reshape(places, model_width), preferred_element_type=jnp.float32
    ).astype(jnp.bfloat16)
    new_gate = jnp.stack(
        [
            jnp.where(second_moved, w_gate[0], arrive_gate),
            jnp.where(second_moved, arrive_gate, w_gate[1]),
        ],
        axis=0,
    )
    new_up = jnp.stack(
        [jnp.where(second_moved, w_up[0], arrive_up), jnp.where(second_moved, arrive_up, w_up[1])],
        axis=0,
    )
    new_down = jnp.stack(
        [
            jnp.where(second_moved, w_down[0], arrive_down),
            jnp.where(second_moved, arrive_down, w_down[1]),
        ],
        axis=0,
    )
    return (moe_output, new_gate, new_up, new_down)


def solution(mesh):
    in_specs = (
        P(("dp", "shard"), None),
        P(("dp", "shard"), None),
        P(("dp", "shard"), None),
        P(),
        P(),
        P("dp", "shard", None),
        P("dp", "shard", None),
        P("dp", "shard", None),
    )
    out_specs = (
        P(("dp", "shard"), None),
        P("dp", "shard", None),
        P("dp", "shard", None),
        P("dp", "shard", None),
    )
    return jax.shard_map(local, mesh=mesh, in_specs=in_specs, out_specs=out_specs, check_vma=False)
```

```python
import jax
import jax.numpy as jnp
from jax import lax
from jax.sharding import PartitionSpec as P


def partner_2(x, axis, apart):
    return lax.ppermute(x, axis, [(i, i ^ 1 << apart) for i in range(lax.axis_size(axis))])


def passed_along(x, axis, by):
    size = lax.axis_size(axis)
    return lax.ppermute(x, axis, [(i, (i + by) % size) for i in range(size)])


def lookup(lookup_keys, lookup_table, entry_count):
    matches = lookup_keys[..., None] == jnp.arange(entry_count, dtype=jnp.int32)
    return jnp.sum(jnp.where(matches, lookup_table, 0), axis=-1)


def widen(pieces, half_count):
    return jnp.tile(pieces, (half_count, 1, 1))


def pair_halves(upper_half, own_rows, other_rows):
    return jnp.where(
        upper_half,
        jnp.stack([other_rows, own_rows], axis=1),
        jnp.stack([own_rows, other_rows], axis=1),
    )


def local(tokens, router_probs, expert_ids, old_place, new_place, w_gate, w_up, w_down):
    slot_count = old_place.shape[0]
    tok_count, top_count = expert_ids.shape
    model_width = tokens.shape[1]
    n_shard = lax.axis_size("shard")
    half_count = n_shard // 2
    column = lax.axis_index("shard")
    row_id = lax.axis_index("dp")
    n_rows = lax.axis_size("dp")
    upper_half = column % 2 == 1
    capacity = max(2, 2 * tok_count * top_count // slot_count)
    places = slot_count * capacity
    core = column % 2
    own = jnp.stack([w_gate, w_up, w_down], axis=1)
    across = partner_2(own, "shard", n_shard.bit_length() - 2)
    first_plane = column < half_count
    by_plane = jnp.where(first_plane, jnp.stack([own, across]), jnp.stack([across, own]))
    kept = jnp.where(core == 0, by_plane[:, 0], by_plane[:, 1])
    handed = jnp.where(core == 0, by_plane[:, 1], by_plane[:, 0])
    received = partner_2(handed, "shard", 0)
    block = jnp.where(
        core == 0, jnp.stack([kept, received], axis=1), jnp.stack([received, kept], axis=1)
    )
    groups = [list(range(g % 2 + (g // 2) * half_count, (g // 2 + 1) * half_count, 2)) for g in range(4)]
    ring = lax.all_gather(block, "shard", axis=0, tiled=False, axis_index_groups=groups)
    full = jnp.transpose(ring, (3, 1, 0, 2, 4, 5)).reshape(3, model_width, -1)
    full_gate, full_up, full_down = full[0], full[1], full[2]
    slot_index = jnp.arange(slot_count, dtype=jnp.int32)
    owner_slot = jnp.sum(
        jnp.where(old_place[None, :] == slot_index[:, None], slot_index[None, :], 0), axis=1
    )
    slot_ids = lookup(expert_ids, owner_slot, slot_count)
    gate_weights = (router_probs / jnp.sum(router_probs, axis=1, keepdims=True)).astype(
        jnp.bfloat16
    )
    side = jnp.concatenate(
        [
            slot_ids.astype(jnp.bfloat16),
            jnp.zeros((tok_count, 128 - top_count), jnp.bfloat16),
        ],
        axis=1,
    )
    ext = jnp.concatenate([tokens, side], axis=1)
    pair = jnp.stack([ext, partner_2(ext, "dp", 0)], axis=0)
    pair = jnp.where(row_id % 2 == 1, pair[::-1], pair)
    groups = [list(range(g, n_rows, 2)) for g in range(2)]
    gathered = lax.all_gather(pair, "dp", axis=0, tiled=True, axis_index_groups=groups)
    gathered = gathered.reshape(n_rows, tok_count, -1)
    gathered_tokens = gathered[..., :model_width]
    gathered_slots = (
        gathered[..., model_width : model_width + top_count].astype(jnp.int32).reshape(n_rows, -1)
    )
    row_slots = 2 * row_id + jnp.arange(2, dtype=jnp.int32)
    in_row = (gathered_slots[:, :, None] == row_slots[None, None, :]).astype(jnp.int32)
    row_rank = jnp.cumsum(in_row, axis=1) - in_row
    picks = (in_row[..., None] == 1) & (
        row_rank[..., None] == jnp.arange(capacity, dtype=jnp.int32)
    )
    picks = picks.reshape(n_rows, tok_count, top_count, 2, capacity)
    picks = jnp.any(picks, axis=2)
    arrived = jnp.einsum(
        "stcr,std->scrd",
        picks.astype(jnp.bfloat16),
        gathered_tokens,
        preferred_element_type=jnp.float32,
    ).astype(jnp.bfloat16)
    own_rows = jnp.where(upper_half, arrived[:, 1], arrived[:, 0])
    other_rows = jnp.where(upper_half, arrived[:, 0], arrived[:, 1])
    partner = partner_2(other_rows, "shard", 0)
    work_rows = jnp.stack([own_rows, partner], axis=0)
    flat_rows = work_rows.reshape(-1, model_width)
    gate_part = jnp.dot(flat_rows, full_gate, preferred_element_type=jnp.float32)
    up_part = jnp.dot(flat_rows, full_up, preferred_element_type=jnp.float32)
    hidden = (jax.nn.silu(gate_part) * up_part).astype(jnp.bfloat16)
    result = lax.dot_general(
        hidden, full_down, (((1,), (1,)), ((), ())), preferred_element_type=jnp.float32
    ).astype(jnp.bfloat16)
    result = result.reshape(2, n_rows, capacity, model_width)
    returned_other = partner_2(result[1], "shard", 0)
    returned = lax.all_to_all(
        pair_halves(upper_half, result[0], returned_other),
        "dp",
        split_axis=0,
        concat_axis=0,
        tiled=True,
    )
    flat_slots = slot_ids.reshape(-1)
    members = (flat_slots[:, None] == slot_index[None, :]).astype(jnp.int32)
    earlier = jnp.cumsum(members, axis=0) - members
    slot_rank = jnp.sum(earlier * members, axis=1)
    position = (flat_slots * capacity + slot_rank).reshape(tok_count, top_count)
    matches = position[:, :, None] == jnp.arange(places, dtype=jnp.int32)[None, None, :]
    combine = jnp.sum(
        jnp.where(matches, gate_weights[:, :, None], jnp.zeros((), jnp.bfloat16)), axis=1
    )
    moe_output = jnp.dot(
        combine, returned.reshape(places, model_width), preferred_element_type=jnp.float32
    ).astype(jnp.bfloat16)
    base_slot = 2 * row_id
    second_old = lax.dynamic_index_in_dim(old_place, base_slot + 1, 0, keepdims=False)
    second_new = lax.dynamic_index_in_dim(new_place, base_slot + 1, 0, keepdims=False)
    second_moved = second_new != second_old
    leave_gate = jnp.where(second_moved, w_gate[1], w_gate[0])
    leave_up = jnp.where(second_moved, w_up[1], w_up[0])
    leave_down = jnp.where(second_moved, w_down[1], w_down[0])
    arrive_gate, arrive_up, arrive_down = passed_along((leave_gate, leave_up, leave_down), "dp", 1)
    new_gate = jnp.stack(
        [
            jnp.where(second_moved, w_gate[0], arrive_gate),
            jnp.where(second_moved, arrive_gate, w_gate[1]),
        ],
        axis=0,
    )
    new_up = jnp.stack(
        [jnp.where(second_moved, w_up[0], arrive_up), jnp.where(second_moved, arrive_up, w_up[1])],
        axis=0,
    )
    new_down = jnp.stack(
        [
            jnp.where(second_moved, w_down[0], arrive_down),
            jnp.where(second_moved, arrive_down, w_down[1]),
        ],
        axis=0,
    )
    return (moe_output, new_gate, new_up, new_down)


def solution(mesh):
    in_specs = (
        P(("dp", "shard"), None),
        P(("dp", "shard"), None),
        P(("dp", "shard"), None),
        P(),
        P(),
        P("dp", "shard", None),
        P("dp", "shard", None),
        P("dp", "shard", None),
    )
    out_specs = (
        P(("dp", "shard"), None),
        P("dp", "shard", None),
        P("dp", "shard", None),
        P("dp", "shard", None),
    )
    return jax.shard_map(local, mesh=mesh, in_specs=in_specs, out_specs=out_specs, check_vma=False)
```

```python
import jax
import jax.numpy as jnp
from jax import lax
from jax.sharding import PartitionSpec as P


def partner_2(x, axis, apart):
    return lax.ppermute(x, axis, [(i, i ^ 1 << apart) for i in range(lax.axis_size(axis))])


def passed_along(x, axis, by):
    size = lax.axis_size(axis)
    return lax.ppermute(x, axis, [(i, (i + by) % size) for i in range(size)])


def lookup(lookup_keys, lookup_table, entry_count):
    matches = lookup_keys[..., None] == jnp.arange(entry_count, dtype=jnp.int32)
    return jnp.sum(jnp.where(matches, lookup_table, 0), axis=-1)


def widen(pieces, half_count):
    return jnp.tile(pieces, (half_count, 1, 1))


def pair_halves(upper_half, own_rows, other_rows):
    return jnp.where(
        upper_half,
        jnp.stack([other_rows, own_rows], axis=1),
        jnp.stack([own_rows, other_rows], axis=1),
    )


def local(tokens, router_probs, expert_ids, old_place, new_place, w_gate, w_up, w_down):
    slot_count = old_place.shape[0]
    tok_count, top_count = expert_ids.shape
    model_width = tokens.shape[1]
    n_shard = lax.axis_size("shard")
    half_count = n_shard // 2
    column = lax.axis_index("shard")
    row_id = lax.axis_index("dp")
    n_rows = lax.axis_size("dp")
    upper_half = column % 2 == 1
    capacity = max(2, 2 * tok_count * top_count // slot_count)
    places = slot_count * capacity
    core = column % 2
    own = jnp.stack([w_gate, w_up, w_down], axis=1)
    across = partner_2(own, "shard", n_shard.bit_length() - 2)
    first_plane = column < half_count
    by_plane = jnp.where(first_plane, jnp.stack([own, across]), jnp.stack([across, own]))
    kept = jnp.where(core == 0, by_plane[:, 0], by_plane[:, 1])
    handed = jnp.where(core == 0, by_plane[:, 1], by_plane[:, 0])
    received = partner_2(handed, "shard", 0)
    block = jnp.where(
        core == 0, jnp.stack([kept, received], axis=1), jnp.stack([received, kept], axis=1)
    )
    groups = [list(range(g % 2 + (g // 2) * half_count, (g // 2 + 1) * half_count, 2)) for g in range(4)]
    ring = lax.all_gather(block, "shard", axis=0, tiled=False, axis_index_groups=groups)
    full = jnp.transpose(ring, (3, 1, 0, 2, 4, 5)).reshape(3, model_width, -1)
    full_gate, full_up, full_down = full[0], full[1], full[2]
    slot_index = jnp.arange(slot_count, dtype=jnp.int32)
    owner_slot = jnp.sum(
        jnp.where(old_place[None, :] == slot_index[:, None], slot_index[None, :], 0), axis=1
    )
    slot_ids = lookup(expert_ids, owner_slot, slot_count)
    gate_weights = (router_probs / jnp.sum(router_probs, axis=1, keepdims=True)).astype(
        jnp.bfloat16
    )
    side = jnp.concatenate(
        [
            slot_ids.astype(jnp.bfloat16),
            jnp.zeros((tok_count, 128 - top_count), jnp.bfloat16),
        ],
        axis=1,
    )
    ext = jnp.concatenate([tokens, side], axis=1)
    pair = jnp.stack([ext, partner_2(ext, "dp", 0)], axis=0)
    pair = jnp.where(row_id % 2 == 1, pair[::-1], pair)
    z_count = n_rows // 2
    ahead = [pair]
    behind = [pair]
    for hop in range(1, z_count // 2 + 1):
        ahead.append(passed_along(ahead[-1], "dp", -2))
        if hop < z_count // 2:
            behind.append(passed_along(behind[-1], "dp", 2))
    by_offset = jnp.stack(ahead + behind[:0:-1], axis=0)
    gathered = jnp.roll(by_offset, row_id // 2, axis=0).reshape(n_rows, tok_count, -1)
    gathered_tokens = gathered[..., :model_width]
    gathered_slots = (
        gathered[..., model_width : model_width + top_count].astype(jnp.int32).reshape(n_rows, -1)
    )
    row_slots = 2 * row_id + jnp.arange(2, dtype=jnp.int32)
    in_row = (gathered_slots[:, :, None] == row_slots[None, None, :]).astype(jnp.int32)
    row_rank = jnp.cumsum(in_row, axis=1) - in_row
    picks = (in_row[..., None] == 1) & (
        row_rank[..., None] == jnp.arange(capacity, dtype=jnp.int32)
    )
    picks = picks.reshape(n_rows, tok_count, top_count, 2, capacity)
    picks = jnp.any(picks, axis=2)
    arrived = jnp.einsum(
        "stcr,std->scrd",
        picks.astype(jnp.bfloat16),
        gathered_tokens,
        preferred_element_type=jnp.float32,
    ).astype(jnp.bfloat16)
    own_rows = jnp.where(upper_half, arrived[:, 1], arrived[:, 0])
    other_rows = jnp.where(upper_half, arrived[:, 0], arrived[:, 1])
    partner = partner_2(other_rows, "shard", 0)
    work_rows = jnp.stack([own_rows, partner], axis=0)
    flat_rows = work_rows.reshape(-1, model_width)
    gate_part = jnp.dot(flat_rows, full_gate, preferred_element_type=jnp.float32)
    up_part = jnp.dot(flat_rows, full_up, preferred_element_type=jnp.float32)
    hidden = (jax.nn.silu(gate_part) * up_part).astype(jnp.bfloat16)
    result = lax.dot_general(
        hidden, full_down, (((1,), (1,)), ((), ())), preferred_element_type=jnp.float32
    ).astype(jnp.bfloat16)
    result = result.reshape(2, n_rows, capacity, model_width)
    returned_other = partner_2(result[1], "shard", 0)
    returned = lax.all_to_all(
        pair_halves(upper_half, result[0], returned_other),
        "dp",
        split_axis=0,
        concat_axis=0,
        tiled=True,
    )
    flat_slots = slot_ids.reshape(-1)
    members = (flat_slots[:, None] == slot_index[None, :]).astype(jnp.int32)
    earlier = jnp.cumsum(members, axis=0) - members
    slot_rank = jnp.sum(earlier * members, axis=1)
    position = (flat_slots * capacity + slot_rank).reshape(tok_count, top_count)
    matches = position[:, :, None] == jnp.arange(places, dtype=jnp.int32)[None, None, :]
    combine = jnp.sum(
        jnp.where(matches, gate_weights[:, :, None], jnp.zeros((), jnp.bfloat16)), axis=1
    )
    moe_output = jnp.dot(
        combine, returned.reshape(places, model_width), preferred_element_type=jnp.float32
    ).astype(jnp.bfloat16)
    base_slot = 2 * row_id
    second_old = lax.dynamic_index_in_dim(old_place, base_slot + 1, 0, keepdims=False)
    second_new = lax.dynamic_index_in_dim(new_place, base_slot + 1, 0, keepdims=False)
    second_moved = second_new != second_old
    leave_gate = jnp.where(second_moved, w_gate[1], w_gate[0])
    leave_up = jnp.where(second_moved, w_up[1], w_up[0])
    leave_down = jnp.where(second_moved, w_down[1], w_down[0])
    arrive_gate, arrive_up, arrive_down = passed_along((leave_gate, leave_up, leave_down), "dp", 1)
    new_gate = jnp.stack(
        [
            jnp.where(second_moved, w_gate[0], arrive_gate),
            jnp.where(second_moved, arrive_gate, w_gate[1]),
        ],
        axis=0,
    )
    new_up = jnp.stack(
        [jnp.where(second_moved, w_up[0], arrive_up), jnp.where(second_moved, arrive_up, w_up[1])],
        axis=0,
    )
    new_down = jnp.stack(
        [
            jnp.where(second_moved, w_down[0], arrive_down),
            jnp.where(second_moved, arrive_down, w_down[1]),
        ],
        axis=0,
    )
    return (moe_output, new_gate, new_up, new_down)


def solution(mesh):
    in_specs = (
        P(("dp", "shard"), None),
        P(("dp", "shard"), None),
        P(("dp", "shard"), None),
        P(),
        P(),
        P("dp", "shard", None),
        P("dp", "shard", None),
        P("dp", "shard", None),
    )
    out_specs = (
        P(("dp", "shard"), None),
        P("dp", "shard", None),
        P("dp", "shard", None),
        P("dp", "shard", None),
    )
    return jax.shard_map(local, mesh=mesh, in_specs=in_specs, out_specs=out_specs, check_vma=False)
```

```python
import jax
import jax.numpy as jnp
from jax import lax
from jax.sharding import PartitionSpec as P


def partner_2(x, axis, apart):
    return lax.ppermute(x, axis, [(i, i ^ 1 << apart) for i in range(lax.axis_size(axis))])


def passed_along(x, axis, by):
    size = lax.axis_size(axis)
    return lax.ppermute(x, axis, [(i, (i + by) % size) for i in range(size)])


def lookup(lookup_keys, lookup_table, entry_count):
    matches = lookup_keys[..., None] == jnp.arange(entry_count, dtype=jnp.int32)
    return jnp.sum(jnp.where(matches, lookup_table, 0), axis=-1)


def widen(pieces, half_count):
    return jnp.tile(pieces, (half_count, 1, 1))


def pair_halves(upper_half, own_rows, other_rows):
    return jnp.where(
        upper_half,
        jnp.stack([other_rows, own_rows], axis=1),
        jnp.stack([own_rows, other_rows], axis=1),
    )


def local(tokens, router_probs, expert_ids, old_place, new_place, w_gate, w_up, w_down):
    slot_count = old_place.shape[0]
    tok_count, top_count = expert_ids.shape
    model_width = tokens.shape[1]
    n_shard = lax.axis_size("shard")
    half_count = n_shard // 2
    column = lax.axis_index("shard")
    row_id = lax.axis_index("dp")
    n_rows = lax.axis_size("dp")
    upper_half = column % 2 == 1
    capacity = max(2, 2 * tok_count * top_count // slot_count)
    places = slot_count * capacity
    core = column % 2
    own = jnp.stack([w_gate, w_up, w_down], axis=1)
    across = partner_2(own, "shard", n_shard.bit_length() - 2)
    first_plane = column < half_count
    by_plane = jnp.where(first_plane, jnp.stack([own, across]), jnp.stack([across, own]))
    kept = jnp.where(core == 0, by_plane[:, 0], by_plane[:, 1])
    handed = jnp.where(core == 0, by_plane[:, 1], by_plane[:, 0])
    received = partner_2(handed, "shard", 0)
    block = jnp.where(
        core == 0, jnp.stack([kept, received], axis=1), jnp.stack([received, kept], axis=1)
    )
    groups = [list(range(g % 2 + (g // 2) * half_count, (g // 2 + 1) * half_count, 2)) for g in range(4)]
    ring = lax.all_gather(block, "shard", axis=0, tiled=False, axis_index_groups=groups)
    full = jnp.transpose(ring, (3, 1, 0, 2, 4, 5)).reshape(3, model_width, -1)
    full_gate, full_up, full_down = full[0], full[1], full[2]
    slot_index = jnp.arange(slot_count, dtype=jnp.int32)
    owner_slot = jnp.sum(
        jnp.where(old_place[None, :] == slot_index[:, None], slot_index[None, :], 0), axis=1
    )
    slot_ids = lookup(expert_ids, owner_slot, slot_count)
    gate_weights = (router_probs / jnp.sum(router_probs, axis=1, keepdims=True)).astype(
        jnp.bfloat16
    )
    side = jnp.concatenate(
        [
            slot_ids.astype(jnp.bfloat16),
            jnp.zeros((tok_count, 128 - top_count), jnp.bfloat16),
        ],
        axis=1,
    )
    ext = jnp.concatenate([tokens, side], axis=1)
    pair = jnp.stack([ext, partner_2(ext, "dp", 0)], axis=0)
    pair = jnp.where(row_id % 2 == 1, pair[::-1], pair)
    z_count = n_rows // 2
    ahead = [pair]
    behind = [pair]
    for hop in range(1, z_count // 2 + 1):
        ahead.append(passed_along(ahead[-1], "dp", -2))
        if hop < z_count // 2:
            behind.append(passed_along(behind[-1], "dp", 2))
    by_offset = jnp.stack(ahead + behind[:0:-1], axis=0)
    gathered = jnp.roll(by_offset, row_id // 2, axis=0).reshape(n_rows, tok_count, -1)
    gathered_tokens = gathered[..., :model_width]
    gathered_slots = (
        gathered[..., model_width : model_width + top_count].astype(jnp.int32).reshape(n_rows, -1)
    )
    row_slots = 2 * row_id + jnp.arange(2, dtype=jnp.int32)
    in_row = (gathered_slots[:, :, None] == row_slots[None, None, :]).astype(jnp.int32)
    row_rank = jnp.cumsum(in_row, axis=1) - in_row
    picks = (in_row[..., None] == 1) & (
        row_rank[..., None] == jnp.arange(capacity, dtype=jnp.int32)
    )
    picks = picks.reshape(n_rows, tok_count, top_count, 2, capacity)
    picks = jnp.any(picks, axis=2)
    arrived = jnp.einsum(
        "stcr,std->scrd",
        picks.astype(jnp.bfloat16),
        gathered_tokens,
        preferred_element_type=jnp.float32,
    ).astype(jnp.bfloat16)
    own_rows = jnp.where(upper_half, arrived[:, 1], arrived[:, 0])
    other_rows = jnp.where(upper_half, arrived[:, 0], arrived[:, 1])
    partner = partner_2(other_rows, "shard", 0)
    work_rows = jnp.stack([own_rows, partner], axis=0)
    base_slot = 2 * row_id
    second_old = lax.dynamic_index_in_dim(old_place, base_slot + 1, 0, keepdims=False)
    second_new = lax.dynamic_index_in_dim(new_place, base_slot + 1, 0, keepdims=False)
    second_moved = second_new != second_old
    leave_gate = jnp.where(second_moved, w_gate[1], w_gate[0])
    leave_up = jnp.where(second_moved, w_up[1], w_up[0])
    leave_down = jnp.where(second_moved, w_down[1], w_down[0])
    arrive_gate, arrive_up, arrive_down = passed_along((leave_gate, leave_up, leave_down), "dp", 1)
    work_rows, arrive_gate, arrive_up, arrive_down = lax.optimization_barrier(
        (work_rows, arrive_gate, arrive_up, arrive_down)
    )
    flat_rows = work_rows.reshape(-1, model_width)
    gate_part = jnp.dot(flat_rows, full_gate, preferred_element_type=jnp.float32)
    up_part = jnp.dot(flat_rows, full_up, preferred_element_type=jnp.float32)
    hidden = (jax.nn.silu(gate_part) * up_part).astype(jnp.bfloat16)
    result = lax.dot_general(
        hidden, full_down, (((1,), (1,)), ((), ())), preferred_element_type=jnp.float32
    ).astype(jnp.bfloat16)
    result = result.reshape(2, n_rows, capacity, model_width)
    returned_other = partner_2(result[1], "shard", 0)
    returned = lax.all_to_all(
        pair_halves(upper_half, result[0], returned_other),
        "dp",
        split_axis=0,
        concat_axis=0,
        tiled=True,
    )
    flat_slots = slot_ids.reshape(-1)
    members = (flat_slots[:, None] == slot_index[None, :]).astype(jnp.int32)
    earlier = jnp.cumsum(members, axis=0) - members
    slot_rank = jnp.sum(earlier * members, axis=1)
    position = (flat_slots * capacity + slot_rank).reshape(tok_count, top_count)
    matches = position[:, :, None] == jnp.arange(places, dtype=jnp.int32)[None, None, :]
    combine = jnp.sum(
        jnp.where(matches, gate_weights[:, :, None], jnp.zeros((), jnp.bfloat16)), axis=1
    )
    moe_output = jnp.dot(
        combine, returned.reshape(places, model_width), preferred_element_type=jnp.float32
    ).astype(jnp.bfloat16)
    new_gate = jnp.stack(
        [
            jnp.where(second_moved, w_gate[0], arrive_gate),
            jnp.where(second_moved, arrive_gate, w_gate[1]),
        ],
        axis=0,
    )
    new_up = jnp.stack(
        [jnp.where(second_moved, w_up[0], arrive_up), jnp.where(second_moved, arrive_up, w_up[1])],
        axis=0,
    )
    new_down = jnp.stack(
        [
            jnp.where(second_moved, w_down[0], arrive_down),
            jnp.where(second_moved, arrive_down, w_down[1]),
        ],
        axis=0,
    )
    return (moe_output, new_gate, new_up, new_down)


def solution(mesh):
    in_specs = (
        P(("dp", "shard"), None),
        P(("dp", "shard"), None),
        P(("dp", "shard"), None),
        P(),
        P(),
        P("dp", "shard", None),
        P("dp", "shard", None),
        P("dp", "shard", None),
    )
    out_specs = (
        P(("dp", "shard"), None),
        P("dp", "shard", None),
        P("dp", "shard", None),
        P("dp", "shard", None),
    )
    return jax.shard_map(local, mesh=mesh, in_specs=in_specs, out_specs=out_specs, check_vma=False)
```

```python
import jax
import jax.numpy as jnp
from jax import lax
from jax.sharding import PartitionSpec as P


def partner_2(x, axis, apart):
    return lax.ppermute(x, axis, [(i, i ^ 1 << apart) for i in range(lax.axis_size(axis))])


def passed_along(x, axis, by):
    size = lax.axis_size(axis)
    return lax.ppermute(x, axis, [(i, (i + by) % size) for i in range(size)])


def lookup(lookup_keys, lookup_table, entry_count):
    matches = lookup_keys[..., None] == jnp.arange(entry_count, dtype=jnp.int32)
    return jnp.sum(jnp.where(matches, lookup_table, 0), axis=-1)


def widen(pieces, half_count):
    return jnp.tile(pieces, (half_count, 1, 1))


def pair_halves(upper_half, own_rows, other_rows):
    return jnp.where(
        upper_half,
        jnp.stack([other_rows, own_rows], axis=1),
        jnp.stack([own_rows, other_rows], axis=1),
    )


def local(tokens, router_probs, expert_ids, old_place, new_place, w_gate, w_up, w_down):
    slot_count = old_place.shape[0]
    tok_count, top_count = expert_ids.shape
    model_width = tokens.shape[1]
    n_shard = lax.axis_size("shard")
    half_count = n_shard // 2
    column = lax.axis_index("shard")
    row_id = lax.axis_index("dp")
    n_rows = lax.axis_size("dp")
    upper_half = column % 2 == 1
    capacity = max(2, 2 * tok_count * top_count // slot_count)
    places = slot_count * capacity
    core = column % 2
    own = jnp.stack([w_gate, w_up, w_down], axis=1)
    across = partner_2(own, "shard", n_shard.bit_length() - 2)
    first_plane = column < half_count
    by_plane = jnp.where(first_plane, jnp.stack([own, across]), jnp.stack([across, own]))
    kept = jnp.where(core == 0, by_plane[:, 0], by_plane[:, 1])
    handed = jnp.where(core == 0, by_plane[:, 1], by_plane[:, 0])
    received = partner_2(handed, "shard", 0)
    block = jnp.where(
        core == 0, jnp.stack([kept, received], axis=1), jnp.stack([received, kept], axis=1)
    )
    groups = [list(range(g % 2 + (g // 2) * half_count, (g // 2 + 1) * half_count, 2)) for g in range(4)]
    ring = lax.all_gather(block, "shard", axis=0, tiled=False, axis_index_groups=groups)
    full = jnp.transpose(ring, (3, 1, 0, 2, 4, 5)).reshape(3, model_width, -1)
    full_gate, full_up, full_down = full[0], full[1], full[2]
    slot_index = jnp.arange(slot_count, dtype=jnp.int32)
    owner_slot = jnp.sum(
        jnp.where(old_place[None, :] == slot_index[:, None], slot_index[None, :], 0), axis=1
    )
    slot_ids = lookup(expert_ids, owner_slot, slot_count)
    gate_weights = (router_probs / jnp.sum(router_probs, axis=1, keepdims=True)).astype(
        jnp.bfloat16
    )
    side = jnp.concatenate(
        [
            slot_ids.astype(jnp.bfloat16),
            jnp.zeros((tok_count, 128 - top_count), jnp.bfloat16),
        ],
        axis=1,
    )
    ext = jnp.concatenate([tokens, side], axis=1)
    pair = jnp.stack([ext, partner_2(ext, "dp", 0)], axis=0)
    pair = jnp.where(row_id % 2 == 1, pair[::-1], pair)
    base_slot = 2 * row_id
    second_old = lax.dynamic_index_in_dim(old_place, base_slot + 1, 0, keepdims=False)
    second_new = lax.dynamic_index_in_dim(new_place, base_slot + 1, 0, keepdims=False)
    second_moved = second_new != second_old
    leave_gate = jnp.where(second_moved, w_gate[1], w_gate[0])
    leave_up = jnp.where(second_moved, w_up[1], w_up[0])
    leave_down = jnp.where(second_moved, w_down[1], w_down[0])
    arrive_gate, arrive_up, arrive_down = passed_along((leave_gate, leave_up, leave_down), "dp", 1)
    z_count = n_rows // 2
    ahead = [pair]
    behind = [pair]
    for hop in range(1, z_count // 2 + 1):
        ahead.append(passed_along(ahead[-1], "dp", -2))
        if hop == 2:
            ahead[-1], arrive_gate, arrive_up, arrive_down = lax.optimization_barrier(
                (ahead[-1], arrive_gate, arrive_up, arrive_down)
            )
        if hop < z_count // 2:
            behind.append(passed_along(behind[-1], "dp", 2))
    by_offset = jnp.stack(ahead + behind[:0:-1], axis=0)
    gathered = jnp.roll(by_offset, row_id // 2, axis=0).reshape(n_rows, tok_count, -1)
    gathered_tokens = gathered[..., :model_width]
    gathered_slots = (
        gathered[..., model_width : model_width + top_count].astype(jnp.int32).reshape(n_rows, -1)
    )
    row_slots = 2 * row_id + jnp.arange(2, dtype=jnp.int32)
    in_row = (gathered_slots[:, :, None] == row_slots[None, None, :]).astype(jnp.int32)
    row_rank = jnp.cumsum(in_row, axis=1) - in_row
    picks = (in_row[..., None] == 1) & (
        row_rank[..., None] == jnp.arange(capacity, dtype=jnp.int32)
    )
    picks = picks.reshape(n_rows, tok_count, top_count, 2, capacity)
    picks = jnp.any(picks, axis=2)
    arrived = jnp.einsum(
        "stcr,std->scrd",
        picks.astype(jnp.bfloat16),
        gathered_tokens,
        preferred_element_type=jnp.float32,
    ).astype(jnp.bfloat16)
    own_rows = jnp.where(upper_half, arrived[:, 1], arrived[:, 0])
    other_rows = jnp.where(upper_half, arrived[:, 0], arrived[:, 1])
    partner = partner_2(other_rows, "shard", 0)
    work_rows = jnp.stack([own_rows, partner], axis=0)
    flat_rows = work_rows.reshape(-1, model_width)
    gate_part = jnp.dot(flat_rows, full_gate, preferred_element_type=jnp.float32)
    up_part = jnp.dot(flat_rows, full_up, preferred_element_type=jnp.float32)
    hidden = (jax.nn.silu(gate_part) * up_part).astype(jnp.bfloat16)
    result = lax.dot_general(
        hidden, full_down, (((1,), (1,)), ((), ())), preferred_element_type=jnp.float32
    ).astype(jnp.bfloat16)
    result = result.reshape(2, n_rows, capacity, model_width)
    returned_other = partner_2(result[1], "shard", 0)
    returned = lax.all_to_all(
        pair_halves(upper_half, result[0], returned_other),
        "dp",
        split_axis=0,
        concat_axis=0,
        tiled=True,
    )
    flat_slots = slot_ids.reshape(-1)
    members = (flat_slots[:, None] == slot_index[None, :]).astype(jnp.int32)
    earlier = jnp.cumsum(members, axis=0) - members
    slot_rank = jnp.sum(earlier * members, axis=1)
    position = (flat_slots * capacity + slot_rank).reshape(tok_count, top_count)
    matches = position[:, :, None] == jnp.arange(places, dtype=jnp.int32)[None, None, :]
    combine = jnp.sum(
        jnp.where(matches, gate_weights[:, :, None], jnp.zeros((), jnp.bfloat16)), axis=1
    )
    moe_output = jnp.dot(
        combine, returned.reshape(places, model_width), preferred_element_type=jnp.float32
    ).astype(jnp.bfloat16)
    new_gate = jnp.stack(
        [
            jnp.where(second_moved, w_gate[0], arrive_gate),
            jnp.where(second_moved, arrive_gate, w_gate[1]),
        ],
        axis=0,
    )
    new_up = jnp.stack(
        [jnp.where(second_moved, w_up[0], arrive_up), jnp.where(second_moved, arrive_up, w_up[1])],
        axis=0,
    )
    new_down = jnp.stack(
        [
            jnp.where(second_moved, w_down[0], arrive_down),
            jnp.where(second_moved, arrive_down, w_down[1]),
        ],
        axis=0,
    )
    return (moe_output, new_gate, new_up, new_down)


def solution(mesh):
    in_specs = (
        P(("dp", "shard"), None),
        P(("dp", "shard"), None),
        P(("dp", "shard"), None),
        P(),
        P(),
        P("dp", "shard", None),
        P("dp", "shard", None),
        P("dp", "shard", None),
    )
    out_specs = (
        P(("dp", "shard"), None),
        P("dp", "shard", None),
        P("dp", "shard", None),
        P("dp", "shard", None),
    )
    return jax.shard_map(local, mesh=mesh, in_specs=in_specs, out_specs=out_specs, check_vma=False)
```

```python
import jax
import jax.numpy as jnp
from jax import lax
from jax.sharding import PartitionSpec as P


def partner_2(x, axis, apart):
    return lax.ppermute(x, axis, [(i, i ^ 1 << apart) for i in range(lax.axis_size(axis))])


def passed_along(x, axis, by):
    size = lax.axis_size(axis)
    return lax.ppermute(x, axis, [(i, (i + by) % size) for i in range(size)])


def lookup(lookup_keys, lookup_table, entry_count):
    matches = lookup_keys[..., None] == jnp.arange(entry_count, dtype=jnp.int32)
    return jnp.sum(jnp.where(matches, lookup_table, 0), axis=-1)


def widen(pieces, half_count):
    return jnp.tile(pieces, (half_count, 1, 1))


def pair_halves(upper_half, own_rows, other_rows):
    return jnp.where(
        upper_half,
        jnp.stack([other_rows, own_rows], axis=1),
        jnp.stack([own_rows, other_rows], axis=1),
    )


def local(tokens, router_probs, expert_ids, old_place, new_place, w_gate, w_up, w_down):
    slot_count = old_place.shape[0]
    tok_count, top_count = expert_ids.shape
    model_width = tokens.shape[1]
    n_shard = lax.axis_size("shard")
    half_count = n_shard // 2
    column = lax.axis_index("shard")
    row_id = lax.axis_index("dp")
    n_rows = lax.axis_size("dp")
    upper_half = column % 2 == 1
    capacity = max(2, 2 * tok_count * top_count // slot_count)
    places = slot_count * capacity
    core = column % 2
    own = jnp.stack([w_gate, w_up, w_down], axis=1)
    across = partner_2(own, "shard", n_shard.bit_length() - 2)
    first_plane = column < half_count
    by_plane = jnp.where(first_plane, jnp.stack([own, across]), jnp.stack([across, own]))
    kept = jnp.where(core == 0, by_plane[:, 0], by_plane[:, 1])
    handed = jnp.where(core == 0, by_plane[:, 1], by_plane[:, 0])
    received = partner_2(handed, "shard", 0)
    block = jnp.where(
        core == 0, jnp.stack([kept, received], axis=1), jnp.stack([received, kept], axis=1)
    )
    groups = [list(range(g % 2 + (g // 2) * half_count, (g // 2 + 1) * half_count, 2)) for g in range(4)]
    block = jnp.transpose(block, (2, 0, 1, 3, 4))
    ring = lax.all_gather(block, "shard", axis=1, tiled=False, axis_index_groups=groups)
    full = ring.reshape(3, model_width, -1)
    full_gate, full_up, full_down = full[0], full[1], full[2]
    slot_index = jnp.arange(slot_count, dtype=jnp.int32)
    owner_slot = jnp.sum(
        jnp.where(old_place[None, :] == slot_index[:, None], slot_index[None, :], 0), axis=1
    )
    slot_ids = lookup(expert_ids, owner_slot, slot_count)
    gate_weights = (router_probs / jnp.sum(router_probs, axis=1, keepdims=True)).astype(
        jnp.bfloat16
    )
    side = jnp.concatenate(
        [
            slot_ids.astype(jnp.bfloat16),
            jnp.zeros((tok_count, 128 - top_count), jnp.bfloat16),
        ],
        axis=1,
    )
    ext = jnp.concatenate([tokens, side], axis=1)
    pair = jnp.stack([ext, partner_2(ext, "dp", 0)], axis=0)
    pair = jnp.where(row_id % 2 == 1, pair[::-1], pair)
    base_slot = 2 * row_id
    second_old = lax.dynamic_index_in_dim(old_place, base_slot + 1, 0, keepdims=False)
    second_new = lax.dynamic_index_in_dim(new_place, base_slot + 1, 0, keepdims=False)
    second_moved = second_new != second_old
    leave_gate = jnp.where(second_moved, w_gate[1], w_gate[0])
    leave_up = jnp.where(second_moved, w_up[1], w_up[0])
    leave_down = jnp.where(second_moved, w_down[1], w_down[0])
    arrive_gate, arrive_up, arrive_down = passed_along((leave_gate, leave_up, leave_down), "dp", 1)
    z_count = n_rows // 2
    ahead = [pair]
    behind = [pair]
    for hop in range(1, z_count // 2 + 1):
        ahead.append(passed_along(ahead[-1], "dp", -2))
        if hop == 2:
            ahead[-1], arrive_gate, arrive_up, arrive_down = lax.optimization_barrier(
                (ahead[-1], arrive_gate, arrive_up, arrive_down)
            )
        if hop < z_count // 2:
            behind.append(passed_along(behind[-1], "dp", 2))
    by_offset = jnp.stack(ahead + behind[:0:-1], axis=0)
    gathered = jnp.roll(by_offset, row_id // 2, axis=0).reshape(n_rows, tok_count, -1)
    gathered_tokens = gathered[..., :model_width]
    gathered_slots = (
        gathered[..., model_width : model_width + top_count].astype(jnp.int32).reshape(n_rows, -1)
    )
    row_slots = 2 * row_id + jnp.arange(2, dtype=jnp.int32)
    in_row = (gathered_slots[:, :, None] == row_slots[None, None, :]).astype(jnp.int32)
    row_rank = jnp.cumsum(in_row, axis=1) - in_row
    picks = (in_row[..., None] == 1) & (
        row_rank[..., None] == jnp.arange(capacity, dtype=jnp.int32)
    )
    picks = picks.reshape(n_rows, tok_count, top_count, 2, capacity)
    picks = jnp.any(picks, axis=2)
    arrived = jnp.einsum(
        "stcr,std->scrd",
        picks.astype(jnp.bfloat16),
        gathered_tokens,
        preferred_element_type=jnp.float32,
    ).astype(jnp.bfloat16)
    own_rows = jnp.where(upper_half, arrived[:, 1], arrived[:, 0])
    other_rows = jnp.where(upper_half, arrived[:, 0], arrived[:, 1])
    partner = partner_2(other_rows, "shard", 0)
    work_rows = jnp.stack([own_rows, partner], axis=0)
    flat_rows = work_rows.reshape(-1, 2, 4, 2, model_width // 16)
    flat_rows = jnp.transpose(flat_rows, (0, 2, 1, 3, 4)).reshape(-1, model_width)
    gate_part = jnp.dot(flat_rows, full_gate, preferred_element_type=jnp.float32)
    up_part = jnp.dot(flat_rows, full_up, preferred_element_type=jnp.float32)
    hidden = (jax.nn.silu(gate_part) * up_part).astype(jnp.bfloat16)
    result = lax.dot_general(
        hidden, full_down, (((1,), (1,)), ((), ())), preferred_element_type=jnp.float32
    ).astype(jnp.bfloat16)
    result = jnp.transpose(result.reshape(-1, 4, 2, 2, model_width // 16), (0, 2, 1, 3, 4))
    result = result.reshape(2, n_rows, capacity, model_width)
    returned_other = partner_2(result[1], "shard", 0)
    returned = lax.all_to_all(
        pair_halves(upper_half, result[0], returned_other),
        "dp",
        split_axis=0,
        concat_axis=0,
        tiled=True,
    )
    flat_slots = slot_ids.reshape(-1)
    members = (flat_slots[:, None] == slot_index[None, :]).astype(jnp.int32)
    earlier = jnp.cumsum(members, axis=0) - members
    slot_rank = jnp.sum(earlier * members, axis=1)
    position = (flat_slots * capacity + slot_rank).reshape(tok_count, top_count)
    matches = position[:, :, None] == jnp.arange(places, dtype=jnp.int32)[None, None, :]
    combine = jnp.sum(
        jnp.where(matches, gate_weights[:, :, None], jnp.zeros((), jnp.bfloat16)), axis=1
    )
    moe_output = jnp.dot(
        combine, returned.reshape(places, model_width), preferred_element_type=jnp.float32
    ).astype(jnp.bfloat16)
    new_gate = jnp.stack(
        [
            jnp.where(second_moved, w_gate[0], arrive_gate),
            jnp.where(second_moved, arrive_gate, w_gate[1]),
        ],
        axis=0,
    )
    new_up = jnp.stack(
        [jnp.where(second_moved, w_up[0], arrive_up), jnp.where(second_moved, arrive_up, w_up[1])],
        axis=0,
    )
    new_down = jnp.stack(
        [
            jnp.where(second_moved, w_down[0], arrive_down),
            jnp.where(second_moved, arrive_down, w_down[1]),
        ],
        axis=0,
    )
    return (moe_output, new_gate, new_up, new_down)


def solution(mesh):
    in_specs = (
        P(("dp", "shard"), None),
        P(("dp", "shard"), None),
        P(("dp", "shard"), None),
        P(),
        P(),
        P("dp", "shard", None),
        P("dp", "shard", None),
        P("dp", "shard", None),
    )
    out_specs = (
        P(("dp", "shard"), None),
        P("dp", "shard", None),
        P("dp", "shard", None),
        P("dp", "shard", None),
    )
    return jax.shard_map(local, mesh=mesh, in_specs=in_specs, out_specs=out_specs, check_vma=False)
```

```python
import jax
import jax.numpy as jnp
from jax import lax
from jax.sharding import PartitionSpec as P


def partner_2(x, axis, apart):
    return lax.ppermute(x, axis, [(i, i ^ 1 << apart) for i in range(lax.axis_size(axis))])


def passed_along(x, axis, by):
    size = lax.axis_size(axis)
    return lax.ppermute(x, axis, [(i, (i + by) % size) for i in range(size)])


def lookup(lookup_keys, lookup_table, entry_count):
    matches = lookup_keys[..., None] == jnp.arange(entry_count, dtype=jnp.int32)
    return jnp.sum(jnp.where(matches, lookup_table, 0), axis=-1)


def widen(pieces, half_count):
    return jnp.tile(pieces, (half_count, 1, 1))


def pair_halves(upper_half, own_rows, other_rows):
    return jnp.where(
        upper_half,
        jnp.stack([other_rows, own_rows], axis=1),
        jnp.stack([own_rows, other_rows], axis=1),
    )


def local(tokens, router_probs, expert_ids, old_place, new_place, w_gate, w_up, w_down):
    slot_count = old_place.shape[0]
    tok_count, top_count = expert_ids.shape
    model_width = tokens.shape[1]
    n_shard = lax.axis_size("shard")
    half_count = n_shard // 2
    column = lax.axis_index("shard")
    row_id = lax.axis_index("dp")
    n_rows = lax.axis_size("dp")
    upper_half = column % 2 == 1
    capacity = max(2, 2 * tok_count * top_count // slot_count)
    places = slot_count * capacity
    core = column % 2
    own = jnp.stack([w_gate, w_up], axis=1)
    across = partner_2(own, "shard", n_shard.bit_length() - 2)
    first_plane = column < half_count
    by_plane = jnp.where(first_plane, jnp.stack([own, across]), jnp.stack([across, own]))
    kept = jnp.where(core == 0, by_plane[:, 0], by_plane[:, 1])
    handed = jnp.where(core == 0, by_plane[:, 1], by_plane[:, 0])
    received = partner_2(handed, "shard", 0)
    block = jnp.where(
        core == 0, jnp.stack([kept, received], axis=1), jnp.stack([received, kept], axis=1)
    )
    groups = [list(range(g % 2 + (g // 2) * half_count, (g // 2 + 1) * half_count, 2)) for g in range(4)]
    ring = lax.all_gather(block, "shard", axis=0, tiled=False, axis_index_groups=groups)
    full = jnp.transpose(ring, (3, 1, 0, 2, 4, 5)).reshape(2, model_width, -1)
    full_gate, full_up = full[0], full[1]
    down_kept = jnp.where(core == 0, w_down[0], w_down[1])
    down_received = partner_2(jnp.where(core == 0, w_down[1], w_down[0]), "shard", 0)
    down_block = jnp.where(
        core == 0,
        jnp.stack([down_kept, down_received]),
        jnp.stack([down_received, down_kept]),
    )
    down_plane = lax.all_gather(down_block, "shard", axis=0, tiled=False, axis_index_groups=groups)
    down_other = partner_2(down_plane, "shard", n_shard.bit_length() - 2)
    full_down = jnp.where(
        first_plane, jnp.stack([down_plane, down_other]), jnp.stack([down_other, down_plane])
    ).reshape(model_width, -1)
    slot_index = jnp.arange(slot_count, dtype=jnp.int32)
    owner_slot = jnp.sum(
        jnp.where(old_place[None, :] == slot_index[:, None], slot_index[None, :], 0), axis=1
    )
    slot_ids = lookup(expert_ids, owner_slot, slot_count)
    gate_weights = (router_probs / jnp.sum(router_probs, axis=1, keepdims=True)).astype(
        jnp.bfloat16
    )
    side = jnp.concatenate(
        [
            slot_ids.astype(jnp.bfloat16),
            jnp.zeros((tok_count, 128 - top_count), jnp.bfloat16),
        ],
        axis=1,
    )
    ext = jnp.concatenate([tokens, side], axis=1)
    pair = jnp.stack([ext, partner_2(ext, "dp", 0)], axis=0)
    pair = jnp.where(row_id % 2 == 1, pair[::-1], pair)
    base_slot = 2 * row_id
    second_old = lax.dynamic_index_in_dim(old_place, base_slot + 1, 0, keepdims=False)
    second_new = lax.dynamic_index_in_dim(new_place, base_slot + 1, 0, keepdims=False)
    second_moved = second_new != second_old
    leave_gate = jnp.where(second_moved, w_gate[1], w_gate[0])
    leave_up = jnp.where(second_moved, w_up[1], w_up[0])
    leave_down = jnp.where(second_moved, w_down[1], w_down[0])
    arrive_gate, arrive_up, arrive_down = passed_along((leave_gate, leave_up, leave_down), "dp", 1)
    z_count = n_rows // 2
    ahead = [pair]
    behind = [pair]
    for hop in range(1, z_count // 2 + 1):
        ahead.append(passed_along(ahead[-1], "dp", -2))
        if hop == 2:
            ahead[-1], arrive_gate, arrive_up, arrive_down = lax.optimization_barrier(
                (ahead[-1], arrive_gate, arrive_up, arrive_down)
            )
        if hop < z_count // 2:
            behind.append(passed_along(behind[-1], "dp", 2))
    by_offset = jnp.stack(ahead + behind[:0:-1], axis=0)
    gathered = jnp.roll(by_offset, row_id // 2, axis=0).reshape(n_rows, tok_count, -1)
    gathered_tokens = gathered[..., :model_width]
    gathered_slots = (
        gathered[..., model_width : model_width + top_count].astype(jnp.int32).reshape(n_rows, -1)
    )
    row_slots = 2 * row_id + jnp.arange(2, dtype=jnp.int32)
    in_row = (gathered_slots[:, :, None] == row_slots[None, None, :]).astype(jnp.int32)
    row_rank = jnp.cumsum(in_row, axis=1) - in_row
    picks = (in_row[..., None] == 1) & (
        row_rank[..., None] == jnp.arange(capacity, dtype=jnp.int32)
    )
    picks = picks.reshape(n_rows, tok_count, top_count, 2, capacity)
    picks = jnp.any(picks, axis=2)
    arrived = jnp.einsum(
        "stcr,std->scrd",
        picks.astype(jnp.bfloat16),
        gathered_tokens,
        preferred_element_type=jnp.float32,
    ).astype(jnp.bfloat16)
    own_rows = jnp.where(upper_half, arrived[:, 1], arrived[:, 0])
    other_rows = jnp.where(upper_half, arrived[:, 0], arrived[:, 1])
    partner = partner_2(other_rows, "shard", 0)
    work_rows = jnp.stack([own_rows, partner], axis=0)
    flat_rows = work_rows.reshape(-1, model_width)
    gate_part = jnp.dot(flat_rows, full_gate, preferred_element_type=jnp.float32)
    up_part = jnp.dot(flat_rows, full_up, preferred_element_type=jnp.float32)
    hidden = (jax.nn.silu(gate_part) * up_part).astype(jnp.bfloat16)
    result = lax.dot_general(
        hidden, full_down, (((1,), (1,)), ((), ())), preferred_element_type=jnp.float32
    ).astype(jnp.bfloat16)
    result = result.reshape(2, n_rows, capacity, model_width)
    returned_other = partner_2(result[1], "shard", 0)
    returned = lax.all_to_all(
        pair_halves(upper_half, result[0], returned_other),
        "dp",
        split_axis=0,
        concat_axis=0,
        tiled=True,
    )
    flat_slots = slot_ids.reshape(-1)
    members = (flat_slots[:, None] == slot_index[None, :]).astype(jnp.int32)
    earlier = jnp.cumsum(members, axis=0) - members
    slot_rank = jnp.sum(earlier * members, axis=1)
    position = (flat_slots * capacity + slot_rank).reshape(tok_count, top_count)
    matches = position[:, :, None] == jnp.arange(places, dtype=jnp.int32)[None, None, :]
    combine = jnp.sum(
        jnp.where(matches, gate_weights[:, :, None], jnp.zeros((), jnp.bfloat16)), axis=1
    )
    moe_output = jnp.dot(
        combine, returned.reshape(places, model_width), preferred_element_type=jnp.float32
    ).astype(jnp.bfloat16)
    new_gate = jnp.stack(
        [
            jnp.where(second_moved, w_gate[0], arrive_gate),
            jnp.where(second_moved, arrive_gate, w_gate[1]),
        ],
        axis=0,
    )
    new_up = jnp.stack(
        [jnp.where(second_moved, w_up[0], arrive_up), jnp.where(second_moved, arrive_up, w_up[1])],
        axis=0,
    )
    new_down = jnp.stack(
        [
            jnp.where(second_moved, w_down[0], arrive_down),
            jnp.where(second_moved, arrive_down, w_down[1]),
        ],
        axis=0,
    )
    return (moe_output, new_gate, new_up, new_down)


def solution(mesh):
    in_specs = (
        P(("dp", "shard"), None),
        P(("dp", "shard"), None),
        P(("dp", "shard"), None),
        P(),
        P(),
        P("dp", "shard", None),
        P("dp", "shard", None),
        P("dp", "shard", None),
    )
    out_specs = (
        P(("dp", "shard"), None),
        P("dp", "shard", None),
        P("dp", "shard", None),
        P("dp", "shard", None),
    )
    return jax.shard_map(local, mesh=mesh, in_specs=in_specs, out_specs=out_specs, check_vma=False)
```

```python
import jax
import jax.numpy as jnp
from jax import lax
from jax.sharding import PartitionSpec as P


def partner_2(x, axis, apart):
    return lax.ppermute(x, axis, [(i, i ^ 1 << apart) for i in range(lax.axis_size(axis))])


def passed_along(x, axis, by):
    size = lax.axis_size(axis)
    return lax.ppermute(x, axis, [(i, (i + by) % size) for i in range(size)])


def lookup(lookup_keys, lookup_table, entry_count):
    matches = lookup_keys[..., None] == jnp.arange(entry_count, dtype=jnp.int32)
    return jnp.sum(jnp.where(matches, lookup_table, 0), axis=-1)


def widen(pieces, half_count):
    return jnp.tile(pieces, (half_count, 1, 1))


def pair_halves(upper_half, own_rows, other_rows):
    return jnp.where(
        upper_half,
        jnp.stack([other_rows, own_rows], axis=1),
        jnp.stack([own_rows, other_rows], axis=1),
    )


def local(tokens, router_probs, expert_ids, old_place, new_place, w_gate, w_up, w_down):
    slot_count = old_place.shape[0]
    tok_count, top_count = expert_ids.shape
    model_width = tokens.shape[1]
    n_shard = lax.axis_size("shard")
    half_count = n_shard // 2
    column = lax.axis_index("shard")
    row_id = lax.axis_index("dp")
    n_rows = lax.axis_size("dp")
    upper_half = column % 2 == 1
    capacity = max(2, 2 * tok_count * top_count // slot_count)
    places = slot_count * capacity
    core = column % 2
    own = jnp.stack([w_gate, w_up, w_down], axis=1)
    across = partner_2(own, "shard", n_shard.bit_length() - 2)
    first_plane = column < half_count
    by_plane = jnp.where(first_plane, jnp.stack([own, across]), jnp.stack([across, own]))
    kept = jnp.where(core == 0, by_plane[:, 0], by_plane[:, 1])
    handed = jnp.where(core == 0, by_plane[:, 1], by_plane[:, 0])
    received = partner_2(handed, "shard", 0)
    block = jnp.where(
        core == 0, jnp.stack([kept, received], axis=1), jnp.stack([received, kept], axis=1)
    )
    groups = [list(range(g % 2 + (g // 2) * half_count, (g // 2 + 1) * half_count, 2)) for g in range(4)]
    ring = lax.all_gather(block[:, :, :2], "shard", axis=0, tiled=False, axis_index_groups=groups)
    full = jnp.transpose(ring, (3, 1, 0, 2, 4, 5)).reshape(2, model_width, -1)
    full_gate, full_up = full[0], full[1]
    down_block, full_gate, full_up = lax.optimization_barrier((block[:, :, 2], full_gate, full_up))
    ring = lax.all_gather(down_block, "shard", axis=0, tiled=False, axis_index_groups=groups)
    full_down = jnp.transpose(ring, (1, 0, 2, 3, 4)).reshape(model_width, -1)
    slot_index = jnp.arange(slot_count, dtype=jnp.int32)
    owner_slot = jnp.sum(
        jnp.where(old_place[None, :] == slot_index[:, None], slot_index[None, :], 0), axis=1
    )
    slot_ids = lookup(expert_ids, owner_slot, slot_count)
    gate_weights = (router_probs / jnp.sum(router_probs, axis=1, keepdims=True)).astype(
        jnp.bfloat16
    )
    side = jnp.concatenate(
        [
            slot_ids.astype(jnp.bfloat16),
            jnp.zeros((tok_count, 128 - top_count), jnp.bfloat16),
        ],
        axis=1,
    )
    ext = jnp.concatenate([tokens, side], axis=1)
    pair = jnp.stack([ext, partner_2(ext, "dp", 0)], axis=0)
    pair = jnp.where(row_id % 2 == 1, pair[::-1], pair)
    base_slot = 2 * row_id
    second_old = lax.dynamic_index_in_dim(old_place, base_slot + 1, 0, keepdims=False)
    second_new = lax.dynamic_index_in_dim(new_place, base_slot + 1, 0, keepdims=False)
    second_moved = second_new != second_old
    leave_gate = jnp.where(second_moved, w_gate[1], w_gate[0])
    leave_up = jnp.where(second_moved, w_up[1], w_up[0])
    leave_down = jnp.where(second_moved, w_down[1], w_down[0])
    arrive_gate, arrive_up, arrive_down = passed_along((leave_gate, leave_up, leave_down), "dp", 1)
    z_count = n_rows // 2
    ahead = [pair]
    behind = [pair]
    for hop in range(1, z_count // 2 + 1):
        ahead.append(passed_along(ahead[-1], "dp", -2))
        if hop == 2:
            ahead[-1], arrive_gate, arrive_up, arrive_down = lax.optimization_barrier(
                (ahead[-1], arrive_gate, arrive_up, arrive_down)
            )
        if hop < z_count // 2:
            behind.append(passed_along(behind[-1], "dp", 2))
    by_offset = jnp.stack(ahead + behind[:0:-1], axis=0)
    gathered = jnp.roll(by_offset, row_id // 2, axis=0).reshape(n_rows, tok_count, -1)
    gathered_tokens = gathered[..., :model_width]
    gathered_slots = (
        gathered[..., model_width : model_width + top_count].astype(jnp.int32).reshape(n_rows, -1)
    )
    row_slots = 2 * row_id + jnp.arange(2, dtype=jnp.int32)
    in_row = (gathered_slots[:, :, None] == row_slots[None, None, :]).astype(jnp.int32)
    row_rank = jnp.cumsum(in_row, axis=1) - in_row
    picks = (in_row[..., None] == 1) & (
        row_rank[..., None] == jnp.arange(capacity, dtype=jnp.int32)
    )
    picks = picks.reshape(n_rows, tok_count, top_count, 2, capacity)
    picks = jnp.any(picks, axis=2)
    arrived = jnp.einsum(
        "stcr,std->scrd",
        picks.astype(jnp.bfloat16),
        gathered_tokens,
        preferred_element_type=jnp.float32,
    ).astype(jnp.bfloat16)
    own_rows = jnp.where(upper_half, arrived[:, 1], arrived[:, 0])
    other_rows = jnp.where(upper_half, arrived[:, 0], arrived[:, 1])
    partner = partner_2(other_rows, "shard", 0)
    work_rows = jnp.stack([own_rows, partner], axis=0)
    flat_rows = work_rows.reshape(-1, model_width)
    gate_part = jnp.dot(flat_rows, full_gate, preferred_element_type=jnp.float32)
    up_part = jnp.dot(flat_rows, full_up, preferred_element_type=jnp.float32)
    hidden = (jax.nn.silu(gate_part) * up_part).astype(jnp.bfloat16)
    result = lax.dot_general(
        hidden, full_down, (((1,), (1,)), ((), ())), preferred_element_type=jnp.float32
    ).astype(jnp.bfloat16)
    result = result.reshape(2, n_rows, capacity, model_width)
    returned_other = partner_2(result[1], "shard", 0)
    returned = lax.all_to_all(
        pair_halves(upper_half, result[0], returned_other),
        "dp",
        split_axis=0,
        concat_axis=0,
        tiled=True,
    )
    flat_slots = slot_ids.reshape(-1)
    members = (flat_slots[:, None] == slot_index[None, :]).astype(jnp.int32)
    earlier = jnp.cumsum(members, axis=0) - members
    slot_rank = jnp.sum(earlier * members, axis=1)
    position = (flat_slots * capacity + slot_rank).reshape(tok_count, top_count)
    matches = position[:, :, None] == jnp.arange(places, dtype=jnp.int32)[None, None, :]
    combine = jnp.sum(
        jnp.where(matches, gate_weights[:, :, None], jnp.zeros((), jnp.bfloat16)), axis=1
    )
    moe_output = jnp.dot(
        combine, returned.reshape(places, model_width), preferred_element_type=jnp.float32
    ).astype(jnp.bfloat16)
    new_gate = jnp.stack(
        [
            jnp.where(second_moved, w_gate[0], arrive_gate),
            jnp.where(second_moved, arrive_gate, w_gate[1]),
        ],
        axis=0,
    )
    new_up = jnp.stack(
        [jnp.where(second_moved, w_up[0], arrive_up), jnp.where(second_moved, arrive_up, w_up[1])],
        axis=0,
    )
    new_down = jnp.stack(
        [
            jnp.where(second_moved, w_down[0], arrive_down),
            jnp.where(second_moved, arrive_down, w_down[1]),
        ],
        axis=0,
    )
    return (moe_output, new_gate, new_up, new_down)


def solution(mesh):
    in_specs = (
        P(("dp", "shard"), None),
        P(("dp", "shard"), None),
        P(("dp", "shard"), None),
        P(),
        P(),
        P("dp", "shard", None),
        P("dp", "shard", None),
        P("dp", "shard", None),
    )
    out_specs = (
        P(("dp", "shard"), None),
        P("dp", "shard", None),
        P("dp", "shard", None),
        P("dp", "shard", None),
    )
    return jax.shard_map(local, mesh=mesh, in_specs=in_specs, out_specs=out_specs, check_vma=False)
```

```python
import jax
import jax.numpy as jnp
from jax import lax
from jax.sharding import PartitionSpec as P


def partner_2(x, axis, apart):
    return lax.ppermute(x, axis, [(i, i ^ 1 << apart) for i in range(lax.axis_size(axis))])


def passed_along(x, axis, by):
    size = lax.axis_size(axis)
    return lax.ppermute(x, axis, [(i, (i + by) % size) for i in range(size)])


def lookup(lookup_keys, lookup_table, entry_count):
    matches = lookup_keys[..., None] == jnp.arange(entry_count, dtype=jnp.int32)
    return jnp.sum(jnp.where(matches, lookup_table, 0), axis=-1)


def widen(pieces, half_count):
    return jnp.tile(pieces, (half_count, 1, 1))


def pair_halves(upper_half, own_rows, other_rows):
    return jnp.where(
        upper_half,
        jnp.stack([other_rows, own_rows], axis=1),
        jnp.stack([own_rows, other_rows], axis=1),
    )


def local(tokens, router_probs, expert_ids, old_place, new_place, w_gate, w_up, w_down):
    slot_count = old_place.shape[0]
    tok_count, top_count = expert_ids.shape
    model_width = tokens.shape[1]
    n_shard = lax.axis_size("shard")
    half_count = n_shard // 2
    column = lax.axis_index("shard")
    row_id = lax.axis_index("dp")
    n_rows = lax.axis_size("dp")
    upper_half = column % 2 == 1
    capacity = max(2, 2 * tok_count * top_count // slot_count)
    places = slot_count * capacity
    core = column % 2
    own = jnp.stack([w_gate, w_up, w_down], axis=1)
    across = partner_2(own, "shard", n_shard.bit_length() - 2)
    first_plane = column < half_count
    by_plane = jnp.where(first_plane, jnp.stack([own, across]), jnp.stack([across, own]))
    kept = jnp.where(core == 0, by_plane[:, 0], by_plane[:, 1])
    handed = jnp.where(core == 0, by_plane[:, 1], by_plane[:, 0])
    received = partner_2(handed, "shard", 0)
    block = jnp.where(
        core == 0, jnp.stack([kept, received], axis=1), jnp.stack([received, kept], axis=1)
    )
    def along_y(x, dy):
        pairs = [
            (i, i - i % half_count + ((i % half_count // 2 + dy) % 4) * 2 + i % 2)
            for i in range(n_shard)
        ]
        return lax.ppermute(x, "shard", pairs)

    from_next = along_y(block, -1)
    from_prev = along_y(block, 1)
    opposite = jnp.stack([along_y(from_next[0], -1), along_y(from_prev[1], 1)])
    by_offset = jnp.stack([block, from_next, opposite, from_prev])
    ring = jnp.roll(by_offset, (column % half_count) // 2, axis=0)
    full = jnp.transpose(ring, (3, 1, 0, 2, 4, 5)).reshape(3, model_width, -1)
    full_gate, full_up, full_down = full[0], full[1], full[2]
    slot_index = jnp.arange(slot_count, dtype=jnp.int32)
    owner_slot = jnp.sum(
        jnp.where(old_place[None, :] == slot_index[:, None], slot_index[None, :], 0), axis=1
    )
    slot_ids = lookup(expert_ids, owner_slot, slot_count)
    gate_weights = (router_probs / jnp.sum(router_probs, axis=1, keepdims=True)).astype(
        jnp.bfloat16
    )
    side = jnp.concatenate(
        [
            slot_ids.astype(jnp.bfloat16),
            jnp.zeros((tok_count, 128 - top_count), jnp.bfloat16),
        ],
        axis=1,
    )
    ext = jnp.concatenate([tokens, side], axis=1)
    pair = jnp.stack([ext, partner_2(ext, "dp", 0)], axis=0)
    pair = jnp.where(row_id % 2 == 1, pair[::-1], pair)
    base_slot = 2 * row_id
    second_old = lax.dynamic_index_in_dim(old_place, base_slot + 1, 0, keepdims=False)
    second_new = lax.dynamic_index_in_dim(new_place, base_slot + 1, 0, keepdims=False)
    second_moved = second_new != second_old
    leave_gate = jnp.where(second_moved, w_gate[1], w_gate[0])
    leave_up = jnp.where(second_moved, w_up[1], w_up[0])
    leave_down = jnp.where(second_moved, w_down[1], w_down[0])
    arrive_gate, arrive_up, arrive_down = passed_along((leave_gate, leave_up, leave_down), "dp", 1)
    z_count = n_rows // 2
    ahead = [pair]
    behind = [pair]
    for hop in range(1, z_count // 2 + 1):
        ahead.append(passed_along(ahead[-1], "dp", -2))
        if hop == 2:
            ahead[-1], arrive_gate, arrive_up, arrive_down = lax.optimization_barrier(
                (ahead[-1], arrive_gate, arrive_up, arrive_down)
            )
        if hop < z_count // 2:
            behind.append(passed_along(behind[-1], "dp", 2))
    by_offset = jnp.stack(ahead + behind[:0:-1], axis=0)
    gathered = jnp.roll(by_offset, row_id // 2, axis=0).reshape(n_rows, tok_count, -1)
    gathered_tokens = gathered[..., :model_width]
    gathered_slots = (
        gathered[..., model_width : model_width + top_count].astype(jnp.int32).reshape(n_rows, -1)
    )
    row_slots = 2 * row_id + jnp.arange(2, dtype=jnp.int32)
    in_row = (gathered_slots[:, :, None] == row_slots[None, None, :]).astype(jnp.int32)
    row_rank = jnp.cumsum(in_row, axis=1) - in_row
    picks = (in_row[..., None] == 1) & (
        row_rank[..., None] == jnp.arange(capacity, dtype=jnp.int32)
    )
    picks = picks.reshape(n_rows, tok_count, top_count, 2, capacity)
    picks = jnp.any(picks, axis=2)
    arrived = jnp.einsum(
        "stcr,std->scrd",
        picks.astype(jnp.bfloat16),
        gathered_tokens,
        preferred_element_type=jnp.float32,
    ).astype(jnp.bfloat16)
    own_rows = jnp.where(upper_half, arrived[:, 1], arrived[:, 0])
    other_rows = jnp.where(upper_half, arrived[:, 0], arrived[:, 1])
    partner = partner_2(other_rows, "shard", 0)
    work_rows = jnp.stack([own_rows, partner], axis=0)
    flat_rows = work_rows.reshape(-1, model_width)
    gate_part = jnp.dot(flat_rows, full_gate, preferred_element_type=jnp.float32)
    up_part = jnp.dot(flat_rows, full_up, preferred_element_type=jnp.float32)
    hidden = (jax.nn.silu(gate_part) * up_part).astype(jnp.bfloat16)
    result = lax.dot_general(
        hidden, full_down, (((1,), (1,)), ((), ())), preferred_element_type=jnp.float32
    ).astype(jnp.bfloat16)
    result = result.reshape(2, n_rows, capacity, model_width)
    returned_other = partner_2(result[1], "shard", 0)
    returned = lax.all_to_all(
        pair_halves(upper_half, result[0], returned_other),
        "dp",
        split_axis=0,
        concat_axis=0,
        tiled=True,
    )
    flat_slots = slot_ids.reshape(-1)
    members = (flat_slots[:, None] == slot_index[None, :]).astype(jnp.int32)
    earlier = jnp.cumsum(members, axis=0) - members
    slot_rank = jnp.sum(earlier * members, axis=1)
    position = (flat_slots * capacity + slot_rank).reshape(tok_count, top_count)
    matches = position[:, :, None] == jnp.arange(places, dtype=jnp.int32)[None, None, :]
    combine = jnp.sum(
        jnp.where(matches, gate_weights[:, :, None], jnp.zeros((), jnp.bfloat16)), axis=1
    )
    moe_output = jnp.dot(
        combine, returned.reshape(places, model_width), preferred_element_type=jnp.float32
    ).astype(jnp.bfloat16)
    new_gate = jnp.stack(
        [
            jnp.where(second_moved, w_gate[0], arrive_gate),
            jnp.where(second_moved, arrive_gate, w_gate[1]),
        ],
        axis=0,
    )
    new_up = jnp.stack(
        [jnp.where(second_moved, w_up[0], arrive_up), jnp.where(second_moved, arrive_up, w_up[1])],
        axis=0,
    )
    new_down = jnp.stack(
        [
            jnp.where(second_moved, w_down[0], arrive_down),
            jnp.where(second_moved, arrive_down, w_down[1]),
        ],
        axis=0,
    )
    return (moe_output, new_gate, new_up, new_down)


def solution(mesh):
    in_specs = (
        P(("dp", "shard"), None),
        P(("dp", "shard"), None),
        P(("dp", "shard"), None),
        P(),
        P(),
        P("dp", "shard", None),
        P("dp", "shard", None),
        P("dp", "shard", None),
    )
    out_specs = (
        P(("dp", "shard"), None),
        P("dp", "shard", None),
        P("dp", "shard", None),
        P("dp", "shard", None),
    )
    return jax.shard_map(local, mesh=mesh, in_specs=in_specs, out_specs=out_specs, check_vma=False)
```

```python
import jax
import jax.numpy as jnp
from jax import lax
from jax.sharding import PartitionSpec as P


def partner_2(x, axis, apart):
    return lax.ppermute(x, axis, [(i, i ^ 1 << apart) for i in range(lax.axis_size(axis))])


def passed_along(x, axis, by):
    size = lax.axis_size(axis)
    return lax.ppermute(x, axis, [(i, (i + by) % size) for i in range(size)])


def lookup(lookup_keys, lookup_table, entry_count):
    matches = lookup_keys[..., None] == jnp.arange(entry_count, dtype=jnp.int32)
    return jnp.sum(jnp.where(matches, lookup_table, 0), axis=-1)


def widen(pieces, half_count):
    return jnp.tile(pieces, (half_count, 1, 1))


def pair_halves(upper_half, own_rows, other_rows):
    return jnp.where(
        upper_half,
        jnp.stack([other_rows, own_rows], axis=1),
        jnp.stack([own_rows, other_rows], axis=1),
    )


def local(tokens, router_probs, expert_ids, old_place, new_place, w_gate, w_up, w_down):
    slot_count = old_place.shape[0]
    tok_count, top_count = expert_ids.shape
    model_width = tokens.shape[1]
    n_shard = lax.axis_size("shard")
    half_count = n_shard // 2
    column = lax.axis_index("shard")
    row_id = lax.axis_index("dp")
    n_rows = lax.axis_size("dp")
    upper_half = column % 2 == 1
    capacity = max(2, 2 * tok_count * top_count // slot_count)
    places = slot_count * capacity
    core = column % 2
    own = jnp.stack([w_gate, w_up, w_down], axis=1)
    across = partner_2(own, "shard", n_shard.bit_length() - 2)
    first_plane = column < half_count
    by_plane = jnp.where(first_plane, jnp.stack([own, across]), jnp.stack([across, own]))
    kept = jnp.where(core == 0, by_plane[:, 0], by_plane[:, 1])
    handed = jnp.where(core == 0, by_plane[:, 1], by_plane[:, 0])
    received = partner_2(handed, "shard", 0)
    block = jnp.where(
        core == 0, jnp.stack([kept, received], axis=1), jnp.stack([received, kept], axis=1)
    )
    groups = [list(range(g % 2 + (g // 2) * half_count, (g // 2 + 1) * half_count, 2)) for g in range(4)]
    ring = lax.all_gather(block, "shard", axis=0, tiled=False, axis_index_groups=groups)
    full = jnp.transpose(ring, (3, 1, 0, 2, 4, 5)).reshape(3, model_width, -1)
    full_gate, full_up, full_down = full[0], full[1], full[2]
    slot_index = jnp.arange(slot_count, dtype=jnp.int32)
    owner_slot = jnp.sum(
        jnp.where(old_place[None, :] == slot_index[:, None], slot_index[None, :], 0), axis=1
    )
    slot_ids = lookup(expert_ids, owner_slot, slot_count)
    gate_weights = (router_probs / jnp.sum(router_probs, axis=1, keepdims=True)).astype(
        jnp.bfloat16
    )
    side = jnp.concatenate(
        [
            slot_ids.astype(jnp.bfloat16),
            jnp.zeros((tok_count, 128 - top_count), jnp.bfloat16),
        ],
        axis=1,
    )
    ext = jnp.concatenate([tokens, side], axis=1)
    pair = jnp.stack([ext, partner_2(ext, "dp", 0)], axis=0)
    pair = jnp.where(row_id % 2 == 1, pair[::-1], pair)
    base_slot = 2 * row_id
    second_old = lax.dynamic_index_in_dim(old_place, base_slot + 1, 0, keepdims=False)
    second_new = lax.dynamic_index_in_dim(new_place, base_slot + 1, 0, keepdims=False)
    second_moved = second_new != second_old
    leave_gate = jnp.where(second_moved, w_gate[1], w_gate[0])
    leave_up = jnp.where(second_moved, w_up[1], w_up[0])
    leave_down = jnp.where(second_moved, w_down[1], w_down[0])
    arrive_gate, arrive_up, arrive_down = passed_along((leave_gate, leave_up, leave_down), "dp", 1)
    z_count = n_rows // 2
    ahead = [pair]
    behind = [pair]
    for hop in range(1, z_count // 2 + 1):
        ahead.append(passed_along(ahead[-1], "dp", -2))
        if hop == 1:
            ahead[-1], arrive_gate, arrive_up, arrive_down = lax.optimization_barrier(
                (ahead[-1], arrive_gate, arrive_up, arrive_down)
            )
        if hop < z_count // 2:
            behind.append(passed_along(behind[-1], "dp", 2))
    by_offset = jnp.stack(ahead + behind[:0:-1], axis=0)
    gathered = jnp.roll(by_offset, row_id // 2, axis=0).reshape(n_rows, tok_count, -1)
    gathered_tokens = gathered[..., :model_width]
    gathered_slots = (
        gathered[..., model_width : model_width + top_count].astype(jnp.int32).reshape(n_rows, -1)
    )
    row_slots = 2 * row_id + jnp.arange(2, dtype=jnp.int32)
    in_row = (gathered_slots[:, :, None] == row_slots[None, None, :]).astype(jnp.int32)
    row_rank = jnp.cumsum(in_row, axis=1) - in_row
    picks = (in_row[..., None] == 1) & (
        row_rank[..., None] == jnp.arange(capacity, dtype=jnp.int32)
    )
    picks = picks.reshape(n_rows, tok_count, top_count, 2, capacity)
    picks = jnp.any(picks, axis=2)
    arrived = jnp.einsum(
        "stcr,std->scrd",
        picks.astype(jnp.bfloat16),
        gathered_tokens,
        preferred_element_type=jnp.float32,
    ).astype(jnp.bfloat16)
    own_rows = jnp.where(upper_half, arrived[:, 1], arrived[:, 0])
    other_rows = jnp.where(upper_half, arrived[:, 0], arrived[:, 1])
    partner = partner_2(other_rows, "shard", 0)
    work_rows = jnp.stack([own_rows, partner], axis=0)
    flat_rows = work_rows.reshape(-1, model_width)
    gate_part = jnp.dot(flat_rows, full_gate, preferred_element_type=jnp.float32)
    up_part = jnp.dot(flat_rows, full_up, preferred_element_type=jnp.float32)
    hidden = (jax.nn.silu(gate_part) * up_part).astype(jnp.bfloat16)
    result = lax.dot_general(
        hidden, full_down, (((1,), (1,)), ((), ())), preferred_element_type=jnp.float32
    ).astype(jnp.bfloat16)
    result = result.reshape(2, n_rows, capacity, model_width)
    returned_other = partner_2(result[1], "shard", 0)
    returned = lax.all_to_all(
        pair_halves(upper_half, result[0], returned_other),
        "dp",
        split_axis=0,
        concat_axis=0,
        tiled=True,
    )
    flat_slots = slot_ids.reshape(-1)
    members = (flat_slots[:, None] == slot_index[None, :]).astype(jnp.int32)
    earlier = jnp.cumsum(members, axis=0) - members
    slot_rank = jnp.sum(earlier * members, axis=1)
    position = (flat_slots * capacity + slot_rank).reshape(tok_count, top_count)
    matches = position[:, :, None] == jnp.arange(places, dtype=jnp.int32)[None, None, :]
    combine = jnp.sum(
        jnp.where(matches, gate_weights[:, :, None], jnp.zeros((), jnp.bfloat16)), axis=1
    )
    moe_output = jnp.dot(
        combine, returned.reshape(places, model_width), preferred_element_type=jnp.float32
    ).astype(jnp.bfloat16)
    new_gate = jnp.stack(
        [
            jnp.where(second_moved, w_gate[0], arrive_gate),
            jnp.where(second_moved, arrive_gate, w_gate[1]),
        ],
        axis=0,
    )
    new_up = jnp.stack(
        [jnp.where(second_moved, w_up[0], arrive_up), jnp.where(second_moved, arrive_up, w_up[1])],
        axis=0,
    )
    new_down = jnp.stack(
        [
            jnp.where(second_moved, w_down[0], arrive_down),
            jnp.where(second_moved, arrive_down, w_down[1]),
        ],
        axis=0,
    )
    return (moe_output, new_gate, new_up, new_down)


def solution(mesh):
    in_specs = (
        P(("dp", "shard"), None),
        P(("dp", "shard"), None),
        P(("dp", "shard"), None),
        P(),
        P(),
        P("dp", "shard", None),
        P("dp", "shard", None),
        P("dp", "shard", None),
    )
    out_specs = (
        P(("dp", "shard"), None),
        P("dp", "shard", None),
        P("dp", "shard", None),
        P("dp", "shard", None),
    )
    return jax.shard_map(local, mesh=mesh, in_specs=in_specs, out_specs=out_specs, check_vma=False)
```

```python
import jax
import jax.numpy as jnp
from jax import lax
from jax.sharding import PartitionSpec as P


def partner_2(x, axis, apart):
    return lax.ppermute(x, axis, [(i, i ^ 1 << apart) for i in range(lax.axis_size(axis))])


def passed_along(x, axis, by):
    size = lax.axis_size(axis)
    return lax.ppermute(x, axis, [(i, (i + by) % size) for i in range(size)])


def lookup(lookup_keys, lookup_table, entry_count):
    matches = lookup_keys[..., None] == jnp.arange(entry_count, dtype=jnp.int32)
    return jnp.sum(jnp.where(matches, lookup_table, 0), axis=-1)


def widen(pieces, half_count):
    return jnp.tile(pieces, (half_count, 1, 1))


def pair_halves(upper_half, own_rows, other_rows):
    return jnp.where(
        upper_half,
        jnp.stack([other_rows, own_rows], axis=1),
        jnp.stack([own_rows, other_rows], axis=1),
    )


def local(tokens, router_probs, expert_ids, old_place, new_place, w_gate, w_up, w_down):
    slot_count = old_place.shape[0]
    tok_count, top_count = expert_ids.shape
    model_width = tokens.shape[1]
    n_shard = lax.axis_size("shard")
    half_count = n_shard // 2
    column = lax.axis_index("shard")
    row_id = lax.axis_index("dp")
    n_rows = lax.axis_size("dp")
    upper_half = column % 2 == 1
    capacity = max(2, 2 * tok_count * top_count // slot_count)
    places = slot_count * capacity
    core = column % 2
    own = jnp.stack([w_gate, w_up, w_down], axis=1)
    across = partner_2(own, "shard", n_shard.bit_length() - 2)
    first_plane = column < half_count
    by_plane = jnp.where(first_plane, jnp.stack([own, across]), jnp.stack([across, own]))
    kept = jnp.where(core == 0, by_plane[:, 0], by_plane[:, 1])
    handed = jnp.where(core == 0, by_plane[:, 1], by_plane[:, 0])
    received = partner_2(handed, "shard", 0)
    block = jnp.where(
        core == 0, jnp.stack([kept, received], axis=1), jnp.stack([received, kept], axis=1)
    )
    groups = [list(range(g % 2 + (g // 2) * half_count, (g // 2 + 1) * half_count, 2)) for g in range(4)]
    ring = lax.all_gather(block, "shard", axis=0, tiled=False, axis_index_groups=groups)
    full = jnp.transpose(ring, (3, 1, 0, 2, 4, 5)).reshape(3, model_width, -1)
    full_gate, full_up, full_down = full[0], full[1], full[2]
    slot_index = jnp.arange(slot_count, dtype=jnp.int32)
    owner_slot = jnp.sum(
        jnp.where(old_place[None, :] == slot_index[:, None], slot_index[None, :], 0), axis=1
    )
    slot_ids = lookup(expert_ids, owner_slot, slot_count)
    gate_weights = (router_probs / jnp.sum(router_probs, axis=1, keepdims=True)).astype(
        jnp.bfloat16
    )
    side = jnp.concatenate(
        [
            slot_ids.astype(jnp.bfloat16),
            jnp.zeros((tok_count, 128 - top_count), jnp.bfloat16),
        ],
        axis=1,
    )
    ext = jnp.concatenate([tokens, side], axis=1)
    pair = jnp.stack([ext, partner_2(ext, "dp", 0)], axis=0)
    pair = jnp.where(row_id % 2 == 1, pair[::-1], pair)
    base_slot = 2 * row_id
    second_old = lax.dynamic_index_in_dim(old_place, base_slot + 1, 0, keepdims=False)
    second_new = lax.dynamic_index_in_dim(new_place, base_slot + 1, 0, keepdims=False)
    second_moved = second_new != second_old
    leave_gate = jnp.where(second_moved, w_gate[1], w_gate[0])
    leave_up = jnp.where(second_moved, w_up[1], w_up[0])
    leave_down = jnp.where(second_moved, w_down[1], w_down[0])
    arrive_gate, arrive_up, arrive_down = passed_along((leave_gate, leave_up, leave_down), "dp", 1)
    z_count = n_rows // 2
    ahead = [pair]
    behind = [pair]
    for hop in range(1, z_count // 2 + 1):
        ahead.append(passed_along(ahead[-1], "dp", -2))
        if hop == 3:
            ahead[-1], arrive_gate, arrive_up, arrive_down = lax.optimization_barrier(
                (ahead[-1], arrive_gate, arrive_up, arrive_down)
            )
        if hop < z_count // 2:
            behind.append(passed_along(behind[-1], "dp", 2))
    by_offset = jnp.stack(ahead + behind[:0:-1], axis=0)
    gathered = jnp.roll(by_offset, row_id // 2, axis=0).reshape(n_rows, tok_count, -1)
    gathered_tokens = gathered[..., :model_width]
    gathered_slots = (
        gathered[..., model_width : model_width + top_count].astype(jnp.int32).reshape(n_rows, -1)
    )
    row_slots = 2 * row_id + jnp.arange(2, dtype=jnp.int32)
    in_row = (gathered_slots[:, :, None] == row_slots[None, None, :]).astype(jnp.int32)
    row_rank = jnp.cumsum(in_row, axis=1) - in_row
    picks = (in_row[..., None] == 1) & (
        row_rank[..., None] == jnp.arange(capacity, dtype=jnp.int32)
    )
    picks = picks.reshape(n_rows, tok_count, top_count, 2, capacity)
    picks = jnp.any(picks, axis=2)
    arrived = jnp.einsum(
        "stcr,std->scrd",
        picks.astype(jnp.bfloat16),
        gathered_tokens,
        preferred_element_type=jnp.float32,
    ).astype(jnp.bfloat16)
    own_rows = jnp.where(upper_half, arrived[:, 1], arrived[:, 0])
    other_rows = jnp.where(upper_half, arrived[:, 0], arrived[:, 1])
    partner = partner_2(other_rows, "shard", 0)
    work_rows = jnp.stack([own_rows, partner], axis=0)
    flat_rows = work_rows.reshape(-1, model_width)
    gate_part = jnp.dot(flat_rows, full_gate, preferred_element_type=jnp.float32)
    up_part = jnp.dot(flat_rows, full_up, preferred_element_type=jnp.float32)
    hidden = (jax.nn.silu(gate_part) * up_part).astype(jnp.bfloat16)
    result = lax.dot_general(
        hidden, full_down, (((1,), (1,)), ((), ())), preferred_element_type=jnp.float32
    ).astype(jnp.bfloat16)
    result = result.reshape(2, n_rows, capacity, model_width)
    returned_other = partner_2(result[1], "shard", 0)
    returned = lax.all_to_all(
        pair_halves(upper_half, result[0], returned_other),
        "dp",
        split_axis=0,
        concat_axis=0,
        tiled=True,
    )
    flat_slots = slot_ids.reshape(-1)
    members = (flat_slots[:, None] == slot_index[None, :]).astype(jnp.int32)
    earlier = jnp.cumsum(members, axis=0) - members
    slot_rank = jnp.sum(earlier * members, axis=1)
    position = (flat_slots * capacity + slot_rank).reshape(tok_count, top_count)
    matches = position[:, :, None] == jnp.arange(places, dtype=jnp.int32)[None, None, :]
    combine = jnp.sum(
        jnp.where(matches, gate_weights[:, :, None], jnp.zeros((), jnp.bfloat16)), axis=1
    )
    moe_output = jnp.dot(
        combine, returned.reshape(places, model_width), preferred_element_type=jnp.float32
    ).astype(jnp.bfloat16)
    new_gate = jnp.stack(
        [
            jnp.where(second_moved, w_gate[0], arrive_gate),
            jnp.where(second_moved, arrive_gate, w_gate[1]),
        ],
        axis=0,
    )
    new_up = jnp.stack(
        [jnp.where(second_moved, w_up[0], arrive_up), jnp.where(second_moved, arrive_up, w_up[1])],
        axis=0,
    )
    new_down = jnp.stack(
        [
            jnp.where(second_moved, w_down[0], arrive_down),
            jnp.where(second_moved, arrive_down, w_down[1]),
        ],
        axis=0,
    )
    return (moe_output, new_gate, new_up, new_down)


def solution(mesh):
    in_specs = (
        P(("dp", "shard"), None),
        P(("dp", "shard"), None),
        P(("dp", "shard"), None),
        P(),
        P(),
        P("dp", "shard", None),
        P("dp", "shard", None),
        P("dp", "shard", None),
    )
    out_specs = (
        P(("dp", "shard"), None),
        P("dp", "shard", None),
        P("dp", "shard", None),
        P("dp", "shard", None),
    )
    return jax.shard_map(local, mesh=mesh, in_specs=in_specs, out_specs=out_specs, check_vma=False)
```
